32 devices in a mesh: cfg: 2 (over y), space: 4 (over z), tm: 4 (over x, core).
Axes of the slice: x: 2, y: 2, z: 4, core: 2. Of those that a mesh axis runs over, the one named last changes fastest.
Arguments:
- eigenvectors: bfloat16 [8, 2, 3, 3072, 384], P(('cfg', 'tm'), None, None, 'space'), parts along dimension 0, may hold values from -6 to 6
- perambulator: bfloat16 [8, 2, 1536, 1536], P(('cfg', 'tm'), None, None, 'space'), parts along dimension 0, may hold values from -0.3125 to 0.3125
- momenta: int32 [2, 3], replicated, may hold values from -2 to 2
- ratios: int32 [2, 2], replicated, may hold values from 1 to 3
- source_slice: int32 [1], replicated, may hold values from 0 to 255
Outputs:
- meson_blocks: float32 [8, 2, 1536, 1536], P(('cfg', 'tm'), None, 'space'), parts along dimension 0
The draws below stay inside these ranges and needn't reach their ends.
There are 2 independent parts, one for each index of `cfg`. The reference program is written for one: setup_inputs(seed, part) draws one part's arguments, and reference() takes and returns one part's arrays. A program takes and returns all parts, laid end to end along the dimension named above; an argument that names none is the same for every part. Nothing has to cross between parts.
Inputs may be any that keep to these rules, and one draw needn't show every extreme that they name: `momenta`: row k is momentum k in units of 2 pi / 64. `ratios`: row k holds the numerator (column 0) and the denominator (column 1) of momentum k's coefficient.
All inputs are finite; a program needn't handle non-finite values.
Results may differ from the reference program's by a relative error of at most 0.0063.
Values may be sent and summed in bfloat16 or wider, within the bound.
No kernel may reach another device: no remote copies, remote signals or barrier semaphores. Data moves between devices by JAX's collectives and lax.ppermute only.
A program may use at most 64 MiB of HBM per device.

```python
import math
import jax
import jax.numpy as jnp
from jax import lax

NVEC = 384
LSIDE = 64
NT = 4
SITES = 3072
ORDER = 1536


def plant(array, stream_key, low, largest):
    shape = array.shape
    place = [jax.random.randint(jax.random.fold_in(stream_key, axis), (), 0, shape[axis]) for axis in range(len(shape))]
    array = array.at[tuple(place)].set(low)
    longest = shape.index(max(shape))
    place[longest] = (place[longest] + 1) % shape[longest]
    return array.at[tuple(place)].set(largest)


def shard_levels(rng, dims, split, least, top_value):
    factor_of = 1.0
    for dim, shards_of in split:
        steps = jax.random.uniform(jax.random.fold_in(jax.random.fold_in(rng, 6), dim), (shards_of,), jnp.float32, least / len(split), top_value / len(split))
        factor_of = factor_of * jnp.repeat(jnp.exp(steps), dims[dim] // shards_of).reshape((-1,) + (1,) * (len(dims) - 1 - dim))
    return factor_of


def normal_values(key, dims, deviation, limit, cuts=(), kind=jnp.bfloat16):
    values = jax.random.normal(key, dims, jnp.float32) * deviation
    if len(cuts) > 0:
        values = shard_levels(key, dims, cuts, -0.22, 0.18) * values
    return jnp.clip(values, min=-limit, max=limit).astype(kind)


def setup_inputs(seed: int = 0, part: int = 0) -> dict:
    key_list = jax.random.split(jax.random.key(seed), 6)
    part_splits = jax.random.split(jax.random.fold_in(key_list[5], part), 6)
    return {
        "eigenvectors": normal_values(part_splits[0], (NT, 2, 3, SITES, NVEC), 1.0, 6.0, ((0, 4), (3, 4))),
        "perambulator": normal_values(part_splits[1], (NT, 2, ORDER, ORDER), NVEC ** -0.5, 0.3125, ((0, 4), (3, 4))),
        "momenta": plant(jax.random.randint(key_list[2], (2, 3), -2, 3), jax.random.fold_in(key_list[2], 1), -2, 2).astype(jnp.int32),
        "ratios": plant(jax.random.randint(key_list[3], (2, 2), 1, 4), jax.random.fold_in(key_list[3], 1), 1, 3).astype(jnp.int32),
        "source_slice": jax.random.randint(key_list[4], (1,), 0, 64 * NT).astype(jnp.int32),
    }


def site_phases(momenta, first_site, site_count):
    site_index = first_site + jnp.arange(site_count, dtype=jnp.int32)
    along_x = site_index % LSIDE
    along_y = site_index // LSIDE % LSIDE
    along_z = site_index // (LSIDE * LSIDE)
    turn_count = momenta[:, 0:1] * along_x[None, :] + momenta[:, 1:2] * along_y[None, :] + momenta[:, 2:3] * along_z[None, :]
    phase_angle = (turn_count % LSIDE).astype(jnp.float32) * (2.0 * math.pi / LSIDE)
    return (jnp.cos(phase_angle), jnp.sin(phase_angle))

def split_elementals(product, vector_count):
    lead_shape = product.shape[:-2]
    product_grid = product.reshape(lead_shape + (2, vector_count, 2, 2, vector_count))
    real_part = product_grid[..., 0, :, :, 0, :] + product_grid[..., 1, :, :, 1, :]
    imaginary = product_grid[..., 0, :, :, 1, :] - product_grid[..., 1, :, :, 0, :]
    stacked = jnp.stack([real_part, imaginary], axis=-4)
    return jnp.moveaxis(stacked, -2, -4)

def elementals(slab, cosine, sine_part):
    color_count, site_count, vector_count = (slab.shape[1], slab.shape[2], slab.shape[3])
    row_count = color_count * site_count
    real_rows = slab[0].reshape(row_count, vector_count)
    imaginary_rows = slab[1].reshape(row_count, vector_count)
    cos_rows = jnp.broadcast_to(cosine[:, None, :], (2, color_count, site_count)).reshape(2, row_count, 1)
    sin_rows = jnp.broadcast_to(sine_part[:, None, :], (2, color_count, site_count)).reshape(2, row_count, 1)
    phased_real = (cos_rows * real_rows[None] + sin_rows * imaginary_rows[None]).astype(jnp.bfloat16)
    phased_imaginary = (cos_rows * imaginary_rows[None] - sin_rows * real_rows[None]).astype(jnp.bfloat16)
    phased = jnp.concatenate([phased_real, phased_imaginary], axis=2)
    phased = jnp.transpose(phased, (1, 0, 2)).reshape(row_count, 4 * vector_count)
    plain_vectors = jnp.concatenate([real_rows, imaginary_rows], axis=1)
    product = jnp.dot(plain_vectors.T, phased, preferred_element_type=jnp.float32)
    return split_elementals(product, vector_count)

def source_block(chosen):
    real_t = chosen[0].T
    imaginary_t = chosen[1].T
    upper = jnp.concatenate([real_t, -imaginary_t], axis=1)
    lower = jnp.concatenate([imaginary_t, real_t], axis=1)
    return jnp.concatenate([upper, lower], axis=0)

def propagate(sink_matrix, tau):
    vector_count = sink_matrix.shape[1]
    spin_count = tau.shape[1] // vector_count
    column_count = tau.shape[2]
    real_part, imaginary = (sink_matrix[0], sink_matrix[1])
    upper = jnp.concatenate([real_part, -imaginary], axis=1)
    lower = jnp.concatenate([imaginary, real_part], axis=1)
    sink_big = jnp.concatenate([upper, lower], axis=0)
    stacked = jnp.transpose(tau.reshape(2, spin_count, vector_count, column_count), (0, 2, 1, 3))
    stacked = stacked.reshape(2 * vector_count, spin_count * column_count)
    product = jnp.dot(sink_big, stacked, preferred_element_type=jnp.float32)
    product = jnp.transpose(product.reshape(2, vector_count, spin_count, column_count), (0, 2, 1, 3))
    return product.reshape(2, spin_count * vector_count, column_count).astype(jnp.bfloat16)

def attach_source(propagated, source_big):
    vector_count = source_big.shape[0] // 2
    row_count = propagated.shape[1]
    spin_count = propagated.shape[2] // vector_count
    stacked = jnp.concatenate([propagated[0].reshape(row_count, spin_count, vector_count), propagated[1].reshape(row_count, spin_count, vector_count)], axis=2)
    product = jnp.dot(stacked.reshape(row_count * spin_count, 2 * vector_count), source_big, preferred_element_type=jnp.float32)
    product = jnp.transpose(product.reshape(row_count, spin_count, 2, vector_count), (2, 0, 1, 3))
    return product.reshape(2, row_count, spin_count * vector_count)

def reference(eigenvectors, perambulator, momenta, ratios, source_slice):
    cosine, sine_part = site_phases(momenta, 0, SITES)
    normalizer = 1.0 / math.sqrt(3 * SITES * NVEC)
    weights = ratios[:, 0].astype(jnp.float32) / ratios[:, 1].astype(jnp.float32) * normalizer

    def sink_of(slab):
        parts = elementals(slab, cosine, sine_part)
        return lax.optimization_barrier(jnp.sum(weights[:, None, None, None] * parts, axis=0)).astype(jnp.bfloat16)
    sink_matrices = lax.map(sink_of, eigenvectors)
    chosen_index = (source_slice[0] % NT).astype(jnp.int32)
    chosen = lax.dynamic_index_in_dim(sink_matrices, chosen_index, 0, keepdims=False)
    source_big = source_block(chosen)

    def slab_result(paired):
        sink_matrix, tau = paired
        return attach_source(propagate(sink_matrix, tau), source_big)
    return lax.map(slab_result, (sink_matrices, perambulator))
```

```python
import functools
import math

import jax
import jax.numpy as jnp
from jax import lax
from jax.experimental import pallas as pl
from jax.experimental.pallas import tpu as pltpu
from jax.sharding import PartitionSpec as P

LSIDE = 64
SPINS = 4


def spread(value, axis, source):
    kept = jnp.where(lax.axis_index(axis) == source, value, 0).astype(value.dtype)
    return lax.psum(kept, axis)


def site_phases(momenta, first_site, site_count):
    site_index = first_site + lax.iota(jnp.int32, site_count)
    along_x = site_index % LSIDE
    along_y = site_index // LSIDE % LSIDE
    along_z = site_index // (LSIDE * LSIDE)
    turn_count = (
        momenta[:, 0:1] * along_x[None, :]
        + momenta[:, 1:2] * along_y[None, :]
        + momenta[:, 2:3] * along_z[None, :]
    )
    phase_angle = (turn_count % LSIDE).astype(jnp.float32) * (2.0 * math.pi / LSIDE)
    return (jnp.cos(phase_angle), jnp.sin(phase_angle))


def split_elementals(product, vector_count):
    lead_shape = product.shape[:-2]
    product_grid = product.reshape(lead_shape + (2, vector_count, 2, 2, vector_count))
    real_part = product_grid[..., 0, :, :, 0, :] + product_grid[..., 1, :, :, 1, :]
    imaginary = product_grid[..., 0, :, :, 1, :] - product_grid[..., 1, :, :, 0, :]
    stacked = jnp.stack([real_part, imaginary], axis=-4)
    return jnp.moveaxis(stacked, -2, -4)


def elementals(vectors, cosine, sine_part):
    slab_count, color_count, site_count, vector_count = (
        vectors.shape[0],
        vectors.shape[2],
        vectors.shape[3],
        vectors.shape[4],
    )
    row_count = color_count * site_count
    real_rows = vectors[:, 0].reshape(slab_count, row_count, vector_count)
    imaginary_rows = vectors[:, 1].reshape(slab_count, row_count, vector_count)
    cos_rows = jnp.broadcast_to(cosine[:, None, :], (2, color_count, site_count)).reshape(
        1, 2, row_count, 1
    )
    sin_rows = jnp.broadcast_to(sine_part[:, None, :], (2, color_count, site_count)).reshape(
        1, 2, row_count, 1
    )
    phased_real = (cos_rows * real_rows[:, None] + sin_rows * imaginary_rows[:, None]).astype(
        jnp.bfloat16
    )
    phased_imaginary = (cos_rows * imaginary_rows[:, None] - sin_rows * real_rows[:, None]).astype(
        jnp.bfloat16
    )
    phased = jnp.concatenate([phased_real, phased_imaginary], axis=3)
    phased = jnp.transpose(phased, (0, 2, 1, 3)).reshape(slab_count, row_count, 4 * vector_count)
    plain_vectors = jnp.concatenate([real_rows, imaginary_rows], axis=2)
    product = lax.dot_general(
        plain_vectors, phased, (((1,), (1,)), ((0,), (0,))), preferred_element_type=jnp.float32
    )
    return split_elementals(product, vector_count)


def source_block(chosen):
    real_t = chosen[0].T
    imaginary_t = chosen[1].T
    upper = jnp.concatenate([real_t, -imaginary_t], axis=1)
    lower = jnp.concatenate([imaginary_t, real_t], axis=1)
    return jnp.concatenate([upper, lower], axis=0)


def propagate(sink_matrix, tau):
    vector_count = sink_matrix.shape[1]
    spin_count = tau.shape[1] // vector_count
    column_count = tau.shape[2]
    real_part, imaginary = (sink_matrix[0], sink_matrix[1])
    upper = jnp.concatenate([real_part, -imaginary], axis=1)
    lower = jnp.concatenate([imaginary, real_part], axis=1)
    sink_big = jnp.concatenate([upper, lower], axis=0)
    stacked = jnp.transpose(tau.reshape(2, spin_count, vector_count, column_count), (0, 2, 1, 3))
    stacked = stacked.reshape(2 * vector_count, spin_count * column_count)
    product = jnp.dot(sink_big, stacked, preferred_element_type=jnp.float32)
    product = jnp.transpose(
        product.reshape(2, vector_count, spin_count, column_count), (0, 2, 1, 3)
    )
    return product.reshape(2, spin_count * vector_count, column_count).astype(jnp.bfloat16)


def attach_source(propagated, source_big):
    vector_count = source_big.shape[0] // 2
    row_count = propagated.shape[1]
    spin_count = propagated.shape[2] // vector_count
    stacked = jnp.concatenate(
        [
            propagated[0].reshape(row_count, spin_count, vector_count),
            propagated[1].reshape(row_count, spin_count, vector_count),
        ],
        axis=2,
    )
    product = jnp.dot(
        stacked.reshape(row_count * spin_count, 2 * vector_count),
        source_big,
        preferred_element_type=jnp.float32,
    )
    product = jnp.transpose(product.reshape(row_count, spin_count, 2, vector_count), (2, 0, 1, 3))
    return product.reshape(2, row_count, spin_count * vector_count)


def general_body(eigenvectors, perambulator, momenta, ratios, source_slice):
    slab_count = eigenvectors.shape[0]
    color_count = eigenvectors.shape[2]
    site_count = eigenvectors.shape[3]
    vector_count = eigenvectors.shape[4]
    first_site = lax.axis_index("space") * site_count
    cosine, sine_part = site_phases(momenta, first_site, site_count)
    normalizer = 1.0 / math.sqrt(color_count * site_count * lax.axis_size("space") * vector_count)
    weights = (
        ratios[:, 0].astype(jnp.float32) / ratios[:, 1].astype(jnp.float32) * normalizer
    ).reshape(1, 2, 1, 1, 1)
    parts = elementals(eigenvectors, cosine, sine_part)
    partial_sums = jnp.sum(weights * parts, axis=1, keepdims=True)
    summed = lax.psum(partial_sums, "space")
    sink_matrices = summed[:, 0].astype(jnp.bfloat16)
    global_slice = source_slice[0] % (slab_count * lax.axis_size("tm"))
    local_source = lax.dynamic_index_in_dim(
        sink_matrices, global_slice % slab_count, 0, keepdims=False
    )
    chosen = spread(local_source, "tm", global_slice // slab_count)
    source_big = source_block(chosen)
    results = []
    for slab in range(slab_count):
        propagated = propagate(sink_matrices[slab], perambulator[slab])[None]
        turned = lax.all_to_all(propagated, "space", split_axis=2, concat_axis=3, tiled=True)
        results.append(attach_source(turned[0], source_big))
    return jnp.stack(results)


def elemental_kernel(info, momenta, weights, v_ref, send_ref, keep_ref, table, phased, total):
    step = pl.program_id(0)
    site_count = v_ref.shape[2]
    n = v_ref.shape[3]
    half = n // 2

    @pl.when(step == 0)
    def _():
        row = lax.broadcasted_iota(jnp.int32, (128, 128), 0)
        lane = lax.broadcasted_iota(jnp.int32, (128, 128), 1)
        second = (row & 1) == 1
        along = [jnp.where(second, momenta[1, a], momenta[0, a]) for a in range(3)]
        shift = jnp.where((row & 2) == 2, LSIDE - LSIDE // 4, 0)
        for tile in range(site_count // 128):
            site = info[0] + tile * 128 + lane
            turn = (
                along[0] * (site % LSIDE)
                + along[1] * (site // LSIDE % LSIDE)
                + along[2] * (site // (LSIDE * LSIDE))
                + shift
            )
            turn = turn & (LSIDE - 1)
            angle = turn.astype(jnp.float32) * (2.0 * math.pi / LSIDE)
            table[pl.ds(tile * 128, 128), :] = jnp.cos(angle).T

    real = v_ref[0, 0].astype(jnp.float32)
    imag = v_ref[1, 0].astype(jnp.float32)
    for k in range(2):
        c = table[:, k : k + 1]
        s = table[:, k + 2 : k + 3]
        phased[:, (2 * k) * n : (2 * k + 1) * n] = (c * real + s * imag).astype(jnp.bfloat16)
        phased[:, (2 * k + 1) * n : (2 * k + 2) * n] = (c * imag - s * real).astype(jnp.bfloat16)
    for part in range(2):
        product = lax.dot_general(
            v_ref[part, 0],
            phased[...],
            (((0,), (0,)), ((), ())),
            preferred_element_type=jnp.float32,
        )
        rows = slice(part * n, (part + 1) * n)

        @pl.when(step == 0)
        def _():
            total[rows, :] = product

        @pl.when(step > 0)
        def _():
            total[rows, :] += product

    @pl.when(step == pl.num_programs(0) - 1)
    def _():
        def rows_of(which):
            upper = pl.multiple_of(which * half, 8)
            lower = pl.multiple_of(n + which * half, 8)
            re = 0.0
            im = 0.0
            for k in range(2):
                w = weights[k]
                zr = slice((2 * k) * n, (2 * k + 1) * n)
                zi = slice((2 * k + 1) * n, (2 * k + 2) * n)
                re += w * (total[pl.ds(upper, half), zr] + total[pl.ds(lower, half), zi])
                im += w * (total[pl.ds(upper, half), zi] - total[pl.ds(lower, half), zr])
            return re, im

        re, im = rows_of(1 - info[1])
        send_ref[0] = re.astype(jnp.bfloat16)
        send_ref[1] = im.astype(jnp.bfloat16)
        re, im = rows_of(info[1])
        keep_ref[0] = re
        keep_ref[1] = im


def elemental_halves(vectors, info, momenta, weights):
    _, color_count, site_count, n = vectors.shape
    half = n // 2
    return pl.pallas_call(
        elemental_kernel,
        grid_spec=pltpu.PrefetchScalarGridSpec(
            num_scalar_prefetch=3,
            grid=(color_count,),
            in_specs=[pl.BlockSpec((2, 1, site_count, n), lambda c, *_: (0, c, 0, 0))],
            out_specs=[
                pl.BlockSpec((2, half, n), lambda c, *_: (0, 0, 0)),
                pl.BlockSpec((2, half, n), lambda c, *_: (0, 0, 0)),
            ],
            scratch_shapes=[
                pltpu.VMEM((site_count, 128), jnp.float32),
                pltpu.VMEM((site_count, 4 * n), jnp.bfloat16),
                pltpu.VMEM((2 * n, 4 * n), jnp.float32),
            ],
        ),
        out_shape=[
            jax.ShapeDtypeStruct((2, half, n), jnp.bfloat16),
            jax.ShapeDtypeStruct((2, half, n), jnp.float32),
        ],
        compiler_params=pltpu.CompilerParams(vmem_limit_bytes=40 * 1024 * 1024),
        name="elementals",
    )(info, momenta, weights, vectors)


def block_kernel(where, sink_ref, source_ref, tau_ref, *rest):
    out_ref = rest[-1]
    rows = sink_ref.shape[1]

    def mul(a, b, dims):
        return lax.dot_general(a, b, (dims, ((), ())), preferred_element_type=jnp.float32)

    nn = ((1,), (0,))
    nt = ((1,), (1,))
    sink = jnp.concatenate([sink_ref[0], sink_ref[1]], axis=0)
    by_re = mul(sink, tau_ref[0], nn)
    by_im = mul(sink, tau_ref[1], nn)
    real = by_re[:rows] - by_im[rows:]
    imag = by_im[:rows] + by_re[rows:]
    prop = jnp.concatenate([real, imag], axis=0).astype(jnp.bfloat16)
    by_re = mul(prop, source_ref[0], nt)
    by_im = mul(prop, source_ref[1], nt)
    out_ref[0, 0] = by_re[:rows] + by_im[rows:]
    out_ref[0, 1] = by_re[rows:] - by_im[:rows]


def block_product(sink, source, tau, place, out, spins):
    n = sink.shape[1]
    rows = n // 2
    in_specs = [
        pl.BlockSpec((2, rows, n), lambda i, w: (0, i, 0)),
        pl.BlockSpec((2, n, n), lambda i, w: (0, 0, 0)),
        pl.BlockSpec((2, n, n), lambda i, w: (0, 0, 0)),
    ]
    args = [sink, source, tau]
    aliases = {}
    if out is not None:
        in_specs.append(pl.BlockSpec(memory_space=pl.ANY))
        args.append(out)
        aliases = {4: 0}
    return pl.pallas_call(
        block_kernel,
        grid_spec=pltpu.PrefetchScalarGridSpec(
            num_scalar_prefetch=1,
            grid=(n // rows,),
            in_specs=in_specs,
            out_specs=pl.BlockSpec((1, 2, rows, n), lambda i, w: (0, 0, i, w[0])),
        ),
        out_shape=jax.ShapeDtypeStruct((1, 2, n, spins * n), jnp.float32),
        input_output_aliases=aliases,
        name="block",
    )(place, *args)


def xor_pairs(count, bit):
    return [(i, i ^ bit) for i in range(count)]


def block_body(eigenvectors, perambulator, momenta, ratios, source_slice):
    color_count, site_count, n = eigenvectors.shape[2:]
    half = n // 2
    quarter = n // 4
    spins = lax.axis_size("space")
    times = lax.axis_size("tm")
    j = lax.axis_index("space")
    low = j % 2
    high = j // 2
    t = lax.axis_index("tm")
    tau = perambulator[0].reshape(2, spins, n, n)

    def block_for(r):
        return lax.dynamic_index_in_dim(tau, j ^ r, 1, keepdims=False)

    def over_space(value, bit):
        return lax.ppermute(value, "space", xor_pairs(spins, bit))

    def over_time(value, bit):
        return lax.ppermute(value, "tm", xor_pairs(times, bit))

    normalizer = 1.0 / math.sqrt(color_count * site_count * spins * n)
    weights = ratios[:, 0].astype(jnp.float32) / ratios[:, 1].astype(jnp.float32) * normalizer
    info = jnp.stack([j * site_count, low]).astype(jnp.int32)

    got = {}
    first = block_for(3)
    got[3, 0] = over_space(first[0], 3)
    send, keep = elemental_halves(eigenvectors[0], info, momenta, weights)

    first_im, send = lax.optimization_barrier((first[1], send))
    half_sum = keep + over_space(send, 1).astype(jnp.float32)
    got[3, 1] = over_space(first_im, 3)
    grid = half_sum.reshape(2, 2, quarter, n)
    give = lax.dynamic_index_in_dim(grid, 1 - high, 1, keepdims=False).astype(jnp.bfloat16)
    mine = lax.dynamic_index_in_dim(grid, high, 1, keepdims=False)
    mine = (mine + over_space(give, 2).astype(jnp.float32)).astype(jnp.bfloat16)
    other = over_space(mine, 2)
    upper = jnp.where(high == 0, mine, other)
    lower = jnp.where(high == 0, other, mine)
    mine = jnp.concatenate([upper, lower], axis=1)
    rest1, rest2, mine = lax.optimization_barrier((block_for(1), block_for(2), mine))
    other = over_space(mine, 1)
    got1 = over_space(rest1, 1)
    got2 = over_space(rest2, 2)
    upper = jnp.where(low == 0, mine, other)
    lower = jnp.where(low == 0, other, mine)
    sink = jnp.concatenate([upper, lower], axis=1)

    chosen_slice = source_slice[0] % times
    partner = over_time(sink, 1)
    here = jnp.where(chosen_slice % 2 == t % 2, sink, partner)
    mine = lax.dynamic_slice_in_dim(here, (t % 2) * half, half, 1)
    far = over_time(mine, 2)
    near = over_time(far, 1)
    upper = jnp.where(t % 2 == 0, far, near)
    lower = jnp.where(t % 2 == 0, near, far)
    away = jnp.concatenate([upper, lower], axis=1)
    source = jnp.where(chosen_slice // 2 == t // 2, here, away)

    def place(r):
        return (j ^ r).reshape(1)

    out = block_product(sink, source, block_for(0), place(0), None, spins)
    got3 = jnp.stack([got[3, 0], got[3, 1]])
    out = block_product(sink, source, got3, place(3), out, spins)
    out = block_product(sink, source, got1, place(1), out, spins)
    out = block_product(sink, source, got2, place(2), out, spins)
    return out


def body(eigenvectors, perambulator, momenta, ratios, source_slice):
    slab_count = eigenvectors.shape[0]
    n = eigenvectors.shape[4]
    space = lax.axis_size("space")
    fits = (
        slab_count == 1
        and space == SPINS
        and lax.axis_size("tm") == 4
        and perambulator.shape[2] == space * n
        and perambulator.shape[3] == n
        and eigenvectors.shape[3] % 128 == 0
        and n % 128 == 0
    )
    chosen = block_body if fits else general_body
    return chosen(eigenvectors, perambulator, momenta, ratios, source_slice)


def solution(mesh):
    placed = (
        P(("cfg", "tm"), None, None, "space", None),
        P(("cfg", "tm"), None, None, "space"),
        P(),
        P(),
        P(),
    )
    return jax.shard_map(
        body,
        mesh=mesh,
        in_specs=placed,
        out_specs=P(("cfg", "tm"), None, "space", None),
        check_vma=False,
    )
```

```python
import math

import jax
import jax.numpy as jnp
from jax import lax
from jax.experimental import pallas as pl
from jax.experimental.pallas import tpu as pltpu
from jax.sharding import PartitionSpec as P


LSIDE = 64
SPINS = 4


def spread(value, axis, source):
    kept = jnp.where(lax.axis_index(axis) == source, value, 0).astype(value.dtype)
    return lax.psum(kept, axis)


def site_phases(momenta, first_site, site_count):
    site_index = first_site + lax.iota(jnp.int32, site_count)
    along_x = site_index % LSIDE
    along_y = site_index // LSIDE % LSIDE
    along_z = site_index // (LSIDE * LSIDE)
    turn_count = (
        momenta[:, 0:1] * along_x[None, :]
        + momenta[:, 1:2] * along_y[None, :]
        + momenta[:, 2:3] * along_z[None, :]
    )
    phase_angle = (turn_count % LSIDE).astype(jnp.float32) * (2.0 * math.pi / LSIDE)
    return (jnp.cos(phase_angle), jnp.sin(phase_angle))


def split_elementals(product, vector_count):
    lead_shape = product.shape[:-2]
    product_grid = product.reshape(lead_shape + (2, vector_count, 2, 2, vector_count))
    real_part = product_grid[..., 0, :, :, 0, :] + product_grid[..., 1, :, :, 1, :]
    imaginary = product_grid[..., 0, :, :, 1, :] - product_grid[..., 1, :, :, 0, :]
    stacked = jnp.stack([real_part, imaginary], axis=-4)
    return jnp.moveaxis(stacked, -2, -4)


def elementals(vectors, cosine, sine_part):
    slab_count, color_count, site_count, vector_count = (
        vectors.shape[0],
        vectors.shape[2],
        vectors.shape[3],
        vectors.shape[4],
    )
    row_count = color_count * site_count
    real_rows = vectors[:, 0].reshape(slab_count, row_count, vector_count)
    imaginary_rows = vectors[:, 1].reshape(slab_count, row_count, vector_count)
    cos_rows = jnp.broadcast_to(cosine[:, None, :], (2, color_count, site_count)).reshape(
        1, 2, row_count, 1
    )
    sin_rows = jnp.broadcast_to(sine_part[:, None, :], (2, color_count, site_count)).reshape(
        1, 2, row_count, 1
    )
    phased_real = (cos_rows * real_rows[:, None] + sin_rows * imaginary_rows[:, None]).astype(
        jnp.bfloat16
    )
    phased_imaginary = (cos_rows * imaginary_rows[:, None] - sin_rows * real_rows[:, None]).astype(
        jnp.bfloat16
    )
    phased = jnp.concatenate([phased_real, phased_imaginary], axis=3)
    phased = jnp.transpose(phased, (0, 2, 1, 3)).reshape(slab_count, row_count, 4 * vector_count)
    plain_vectors = jnp.concatenate([real_rows, imaginary_rows], axis=2)
    product = lax.dot_general(
        plain_vectors, phased, (((1,), (1,)), ((0,), (0,))), preferred_element_type=jnp.float32
    )
    return split_elementals(product, vector_count)


def source_block(chosen):
    real_t = chosen[0].T
    imaginary_t = chosen[1].T
    upper = jnp.concatenate([real_t, -imaginary_t], axis=1)
    lower = jnp.concatenate([imaginary_t, real_t], axis=1)
    return jnp.concatenate([upper, lower], axis=0)


def propagate(sink_matrix, tau):
    vector_count = sink_matrix.shape[1]
    spin_count = tau.shape[1] // vector_count
    column_count = tau.shape[2]
    real_part, imaginary = (sink_matrix[0], sink_matrix[1])
    upper = jnp.concatenate([real_part, -imaginary], axis=1)
    lower = jnp.concatenate([imaginary, real_part], axis=1)
    sink_big = jnp.concatenate([upper, lower], axis=0)
    stacked = jnp.transpose(tau.reshape(2, spin_count, vector_count, column_count), (0, 2, 1, 3))
    stacked = stacked.reshape(2 * vector_count, spin_count * column_count)
    product = jnp.dot(sink_big, stacked, preferred_element_type=jnp.float32)
    product = jnp.transpose(
        product.reshape(2, vector_count, spin_count, column_count), (0, 2, 1, 3)
    )
    return product.reshape(2, spin_count * vector_count, column_count).astype(jnp.bfloat16)


def attach_source(propagated, source_big):
    vector_count = source_big.shape[0] // 2
    row_count = propagated.shape[1]
    spin_count = propagated.shape[2] // vector_count
    stacked = jnp.concatenate(
        [
            propagated[0].reshape(row_count, spin_count, vector_count),
            propagated[1].reshape(row_count, spin_count, vector_count),
        ],
        axis=2,
    )
    product = jnp.dot(
        stacked.reshape(row_count * spin_count, 2 * vector_count),
        source_big,
        preferred_element_type=jnp.float32,
    )
    product = jnp.transpose(product.reshape(row_count, spin_count, 2, vector_count), (2, 0, 1, 3))
    return product.reshape(2, row_count, spin_count * vector_count)


def general_body(eigenvectors, perambulator, momenta, ratios, source_slice):
    slab_count = eigenvectors.shape[0]
    color_count = eigenvectors.shape[2]
    site_count = eigenvectors.shape[3]
    vector_count = eigenvectors.shape[4]
    first_site = lax.axis_index("space") * site_count
    cosine, sine_part = site_phases(momenta, first_site, site_count)
    normalizer = 1.0 / math.sqrt(color_count * site_count * lax.axis_size("space") * vector_count)
    weights = (
        ratios[:, 0].astype(jnp.float32) / ratios[:, 1].astype(jnp.float32) * normalizer
    ).reshape(1, 2, 1, 1, 1)
    parts = elementals(eigenvectors, cosine, sine_part)
    partial_sums = jnp.sum(weights * parts, axis=1, keepdims=True)
    summed = lax.psum(partial_sums, "space")
    sink_matrices = summed[:, 0].astype(jnp.bfloat16)
    global_slice = source_slice[0] % (slab_count * lax.axis_size("tm"))
    local_source = lax.dynamic_index_in_dim(
        sink_matrices, global_slice % slab_count, 0, keepdims=False
    )
    chosen = spread(local_source, "tm", global_slice // slab_count)
    source_big = source_block(chosen)
    results = []
    for slab in range(slab_count):
        propagated = propagate(sink_matrices[slab], perambulator[slab])[None]
        turned = lax.all_to_all(propagated, "space", split_axis=2, concat_axis=3, tiled=True)
        results.append(attach_source(turned[0], source_big))
    return jnp.stack(results)


HBM = pl.BlockSpec(memory_space=pltpu.MemorySpace.HBM)


def pick_kernel(tau_hbm, out_hbm, buffer, in_sems, out_sems):
    which = lax.axis_index("space") ^ 3
    loads = [
        pltpu.make_async_copy(tau_hbm.at[part, which], buffer.at[part], in_sems.at[part])
        for part in range(2)
    ]
    stores = [
        pltpu.make_async_copy(buffer.at[part], out_hbm.at[part], out_sems.at[part])
        for part in range(2)
    ]
    for copy in loads:
        copy.start()
    for load, store in zip(loads, stores):
        load.wait()
        store.start()
    for copy in stores:
        copy.wait()


def pick_block(tau):
    _, _, n, columns = tau.shape
    return pl.pallas_call(
        pick_kernel,
        in_specs=[HBM],
        out_specs=HBM,
        scratch_shapes=[
            pltpu.VMEM((2, n, columns), tau.dtype),
            pltpu.SemaphoreType.DMA((2,)),
            pltpu.SemaphoreType.DMA((2,)),
        ],
        out_shape=jax.ShapeDtypeStruct((2, n, columns), tau.dtype),
        name="pick",
    )(tau)


def elemental_kernel(
    momenta,
    ratios,
    v_hbm,
    tau_hbm,
    rounded_a,
    rounded_b,
    full_a,
    full_b,
    by1,
    by2,
    vectors,
    blocks,
    table,
    phased,
    total,
    sems,
    in_sems,
    out_sems,
):
    place = lax.axis_index("space")
    colors = v_hbm.shape[1]
    site_count = v_hbm.shape[2]
    n = v_hbm.shape[3]
    half = n // 2
    loads = [
        pltpu.make_async_copy(v_hbm.at[:, c], vectors.at[c], sems.at[c]) for c in range(colors)
    ]
    fetches = [
        pltpu.make_async_copy(tau_hbm.at[:, place ^ r], blocks.at[r - 1], in_sems.at[r - 1])
        for r in (1, 2)
    ]
    stores = [
        pltpu.make_async_copy(blocks.at[i], out, out_sems.at[i]) for i, out in enumerate((by1, by2))
    ]
    for copy in loads + fetches:
        copy.start()

    row = lax.broadcasted_iota(jnp.int32, (8, 128), 0)
    lane = lax.broadcasted_iota(jnp.int32, (8, 128), 1)
    second = (row & 1) == 1
    along = [jnp.where(second, momenta[1, a], momenta[0, a]) for a in range(3)]
    shift = jnp.where((row & 2) == 2, LSIDE - LSIDE // 4, 0)
    for tile in range(site_count // 128):
        site = place * site_count + tile * 128 + lane
        turn = (
            along[0] * (site % LSIDE)
            + along[1] * (site // LSIDE % LSIDE)
            + along[2] * (site // (LSIDE * LSIDE))
            + shift
        )
        turn = turn & (LSIDE - 1)
        angle = turn.astype(jnp.float32) * (2.0 * math.pi / LSIDE)
        table[pl.ds(tile * 128, 128), 0:8] = jnp.cos(angle).T

    def phase(color, k):
        slot = (2 * color + k) % 2
        real = vectors[color, 0].astype(jnp.float32)
        imag = vectors[color, 1].astype(jnp.float32)
        c = table[:, k : k + 1]
        s = table[:, k + 2 : k + 3]
        phased[slot, :, 0:n] = (c * real + s * imag).astype(jnp.bfloat16)
        phased[slot, :, n : 2 * n] = (c * imag - s * real).astype(jnp.bfloat16)

    def multiply(color, k):
        slot = (2 * color + k) % 2
        cols = slice(2 * k * n, (2 * k + 2) * n)
        for part in range(2):
            product = lax.dot_general(
                vectors[color, part],
                phased[slot],
                (((0,), (0,)), ((), ())),
                preferred_element_type=jnp.float32,
            )
            rows = slice(part * n, (part + 1) * n)
            if color == 0:
                total[rows, cols] = product
            else:
                total[rows, cols] += product

    before = None
    for color in range(colors):
        loads[color].wait()
        for k in range(2):
            phase(color, k)
            if before is not None:
                multiply(*before)
            before = (color, k)
        if color == 1:
            for copy in fetches:
                copy.wait()
            for copy in stores:
                copy.start()
    multiply(*before)

    normalizer = 1.0 / math.sqrt(colors * site_count * lax.axis_size("space") * n)
    re = 0.0
    im = 0.0
    for k in range(2):
        ratio = [jnp.full((8, 128), ratios[k, i], jnp.int32).astype(jnp.float32) for i in range(2)]
        w = (ratio[0] / ratio[1] * normalizer)[0:1, 0:1]
        zr = slice((2 * k) * n, (2 * k + 1) * n)
        zi = slice((2 * k + 1) * n, (2 * k + 2) * n)
        re += w * (total[0:n, zr] + total[n : 2 * n, zi])
        im += w * (total[0:n, zi] - total[n : 2 * n, zr])
    for part, value in enumerate((re, im)):
        small = value.astype(jnp.bfloat16)
        rounded_a[part] = small[:half]
        rounded_b[part] = small[half:]
        full_a[part] = value[:half]
        full_b[part] = value[half:]
    for copy in stores:
        copy.wait()


def elemental_sums(vectors, tau, momenta, ratios):
    _, color_count, site_count, n = vectors.shape
    half = n // 2
    rows = pl.BlockSpec((2, half, n), lambda i, *_: (0, 0, 0))
    return pl.pallas_call(
        elemental_kernel,
        grid_spec=pltpu.PrefetchScalarGridSpec(
            num_scalar_prefetch=2,
            grid=(1,),
            in_specs=[HBM, HBM],
            out_specs=[rows] * 4 + [HBM] * 2,
            scratch_shapes=[
                pltpu.VMEM((color_count, 2, site_count, n), jnp.bfloat16),
                pltpu.VMEM((2, 2, n, n), jnp.bfloat16),
                pltpu.VMEM((site_count, 128), jnp.float32),
                pltpu.VMEM((2, site_count, 2 * n), jnp.bfloat16),
                pltpu.VMEM((2 * n, 4 * n), jnp.float32),
                pltpu.SemaphoreType.DMA((color_count,)),
                pltpu.SemaphoreType.DMA((2,)),
                pltpu.SemaphoreType.DMA((2,)),
            ],
        ),
        out_shape=[
            jax.ShapeDtypeStruct((2, rows_of, n), dtype)
            for rows_of, dtype in (
                (half, jnp.bfloat16),
                (half, jnp.bfloat16),
                (half, jnp.float32),
                (half, jnp.float32),
                (n, jnp.bfloat16),
                (n, jnp.bfloat16),
            )
        ],
        compiler_params=pltpu.CompilerParams(vmem_limit_bytes=40 * 1024 * 1024),
        name="elementals",
    )(momenta, ratios, vectors, tau)


def complex_rows(real, imag):
    upper = jnp.concatenate([real, imag], axis=1)
    lower = jnp.concatenate([-imag, real], axis=1)
    return jnp.concatenate([upper, lower], axis=0)


def sandwich(sink, tau_re, tau_im, source):
    prop = jnp.dot(sink, complex_rows(tau_re, tau_im), preferred_element_type=jnp.float32)
    return lax.dot_general(
        prop.astype(jnp.bfloat16),
        source,
        (((1,), (1,)), ((), ())),
        preferred_element_type=jnp.float32,
    )


def copy_if(flag, first, second, target, sem):
    @pl.when(flag == 1)
    def _():
        pltpu.make_async_copy(first, target, sem).start()

    @pl.when(flag != 1)
    def _():
        pltpu.make_async_copy(second, target, sem).start()


def is_inner(place):
    return jnp.where((place == 1) | (place == 2), 1, 0)


def three_kernel(source_slice, *refs):
    (sum_a, sum_b, out_a, out_b, here_a, here_b, far_a, far_b, beside_a, beside_b) = refs[:10]
    tau_hbm, got_n, got_b, got_c = refs[10:14]
    out_hbm, sink_out, source_out = refs[14:17]
    sink, source, blocks, staged, sink_sems, source_sems, block_sems, out_sems = refs[17:]
    n = sink_out.shape[0]
    half = n // 2
    quarter = n // 4
    place = lax.axis_index("space")
    time = lax.axis_index("tm")
    inner = is_inner(place)
    same = jnp.where(source_slice[0] % lax.axis_size("tm") // 2 == time // 2, 1, 0)
    odd = time % 2

    for i, (mine, got) in enumerate(((sum_a, out_a), (sum_b, out_b))):
        copy_if(inner, mine, got, sink.at[:, pl.ds(i * half, half)], sink_sems.at[i])
    pltpu.make_async_copy(tau_hbm.at[:, place], blocks.at[0], block_sems.at[0]).start()
    pltpu.make_async_copy(got_n, blocks.at[1], block_sems.at[1]).start()
    for i, (here, far, beside) in enumerate(
        ((here_a, far_a, beside_a), (here_b, far_b, beside_b))
    ):
        rows = source.at[:, pl.ds(i * half, half)]

        @pl.when(same == 1)
        def _():
            first, second = pl.ds(0, quarter), pl.ds(quarter, quarter)
            pltpu.make_async_copy(here.at[:, first], rows.at[:, first], source_sems.at[2 * i]).start()
            pltpu.make_async_copy(
                here.at[:, second], rows.at[:, second], source_sems.at[2 * i + 1]
            ).start()

        @pl.when(same != 1)
        def _():
            mine = pl.multiple_of(odd * quarter, 16)
            other = pl.multiple_of((1 - odd) * quarter, 16)
            pltpu.make_async_copy(
                far, rows.at[:, pl.ds(mine, quarter)], source_sems.at[2 * i]
            ).start()
            pltpu.make_async_copy(
                beside, rows.at[:, pl.ds(other, quarter)], source_sems.at[2 * i + 1]
            ).start()

    copy_if(inner, got_b, got_c, blocks.at[2], block_sems.at[2])

    for i, got in enumerate((out_a, out_b)):
        pltpu.make_async_copy(got, sink.at[:, pl.ds(i * half, half)], sink_sems.at[i]).wait()
    sink_rows = jnp.concatenate([sink[0], sink[1]], axis=1)
    sink_out[...] = sink_rows
    for i in range(2):
        for q in range(2):
            pltpu.make_async_copy(
                far_a, source.at[:, pl.ds(0, quarter)], source_sems.at[2 * i + q]
            ).wait()
    source_rows = complex_rows(source[0], source[1])
    source_out[...] = source_rows

    stores = []
    for i in range(3):
        pltpu.make_async_copy(got_n, blocks.at[i], block_sems.at[i]).wait()
        product = sandwich(sink_rows, blocks[i, 0], blocks[i, 1], source_rows)
        staged[i, 0] = product[:, :n]
        staged[i, 1] = product[:, n:]
        column = pl.multiple_of((place ^ i) * n, 128)
        store = pltpu.make_async_copy(
            staged.at[i], out_hbm.at[0, :, :, pl.ds(column, n)], out_sems.at[i]
        )
        store.start()
        stores.append(store)
    for store in stores:
        store.wait()


def three_blocks(source_slice, pieces, tau, got, spins):
    n = tau.shape[2]
    return pl.pallas_call(
        three_kernel,
        grid_spec=pltpu.PrefetchScalarGridSpec(
            num_scalar_prefetch=1,
            grid=(1,),
            in_specs=[HBM] * 14,
            out_specs=[
                HBM,
                pl.BlockSpec((n, 2 * n), lambda i, *_: (0, 0)),
                pl.BlockSpec((2 * n, 2 * n), lambda i, *_: (0, 0)),
            ],
            scratch_shapes=[
                pltpu.VMEM((2, n, n), jnp.bfloat16),
                pltpu.VMEM((2, n, n), jnp.bfloat16),
                pltpu.VMEM((3, 2, n, n), jnp.bfloat16),
                pltpu.VMEM((3, 2, n, n), jnp.float32),
                pltpu.SemaphoreType.DMA((2,)),
                pltpu.SemaphoreType.DMA((4,)),
                pltpu.SemaphoreType.DMA((3,)),
                pltpu.SemaphoreType.DMA((3,)),
            ],
        ),
        out_shape=[
            jax.ShapeDtypeStruct((1, 2, n, spins * n), jnp.float32),
            jax.ShapeDtypeStruct((n, 2 * n), jnp.bfloat16),
            jax.ShapeDtypeStruct((2 * n, 2 * n), jnp.bfloat16),
        ],
        compiler_params=pltpu.CompilerParams(vmem_limit_bytes=40 * 1024 * 1024),
        name="three",
    )(source_slice, *pieces, tau, *got)


def last_kernel(sink, source, got_a, got_d, _, out_hbm, block, staged, sem, out_sem):
    n = sink.shape[0]
    place = lax.axis_index("space")
    copy_if(is_inner(place), got_a, got_d, block, sem)
    pltpu.make_async_copy(got_a, block, sem).wait()
    product = sandwich(sink[...], block[0], block[1], source[...])
    staged[0] = product[:, :n]
    staged[1] = product[:, n:]
    column = pl.multiple_of((place ^ 3) * n, 128)
    store = pltpu.make_async_copy(staged, out_hbm.at[0, :, :, pl.ds(column, n)], out_sem)
    store.start()
    store.wait()


def last_block(sink, source, got_a, got_d, out):
    n = sink.shape[0]
    return pl.pallas_call(
        last_kernel,
        grid=(1,),
        in_specs=[
            pl.BlockSpec((n, 2 * n), lambda i: (0, 0)),
            pl.BlockSpec((2 * n, 2 * n), lambda i: (0, 0)),
            HBM,
            HBM,
            HBM,
        ],
        out_specs=HBM,
        scratch_shapes=[
            pltpu.VMEM((2, n, n), jnp.bfloat16),
            pltpu.VMEM((2, n, n), jnp.float32),
            pltpu.SemaphoreType.DMA,
            pltpu.SemaphoreType.DMA,
        ],
        out_shape=jax.ShapeDtypeStruct(out.shape, out.dtype),
        input_output_aliases={4: 0},
        compiler_params=pltpu.CompilerParams(vmem_limit_bytes=40 * 1024 * 1024),
        name="last",
    )(sink, source, got_a, got_d, out)


def block_body(eigenvectors, perambulator, momenta, ratios, source_slice):
    return ordered_body(eigenvectors, perambulator, momenta, ratios, source_slice)


def ordered_body(eigenvectors, perambulator, momenta, ratios, source_slice):
    n = eigenvectors.shape[4]
    quarter = n // 4
    spins = lax.axis_size("space")
    j = lax.axis_index("space")
    inner = (j == 1) | (j == 2)
    odd = lax.axis_index("tm") % 2
    tau = perambulator[0].reshape(2, spins, n, n)

    def move(value, pairs, axis="space"):
        return lax.ppermute(value, axis, pairs)

    middle = [(1, 2), (2, 1)]
    ends = [(0, 3), (3, 0)]
    inward = [(0, 1), (3, 2)]
    outward = [(1, 0), (2, 3)]
    skip_in = [(0, 2), (3, 1)]
    skip_out = [(1, 3), (2, 0)]
    core = [(0, 1), (1, 0), (2, 3), (3, 2)]
    chip = [(0, 2), (2, 0), (1, 3), (3, 1)]

    by3 = pick_block(tau)
    got_a = move(by3, middle)
    rounded_a, rounded_b, full_a, full_b, by1, by2 = elemental_sums(
        eigenvectors[0], tau, momenta, ratios
    )
    got_n = move(by1, inward + outward)
    got_c = move(by2, skip_out)
    got_b = move(by2, skip_in)
    got_d = move(by3, ends)

    pieces = []
    for rounded, full in ((rounded_a, full_a), (rounded_b, full_b)):
        inside = move(rounded, inward)
        pair = full + inside.astype(jnp.float32)
        across = move(pair.astype(jnp.bfloat16), middle)
        summed = (pair + across.astype(jnp.float32)).astype(jnp.bfloat16)
        outside = move(summed, outward)
        sink = jnp.where(inner, summed, outside)
        partner = move(sink, core, "tm")
        here = jnp.where(source_slice[0] % 2 == odd, sink, partner)
        mine = lax.dynamic_slice_in_dim(here, odd * quarter, quarter, 1)
        far = move(mine, chip, "tm")
        beside = move(far, core, "tm")
        pieces.append((summed, outside, here, far, beside))
    pieces = [piece for pair in zip(*pieces) for piece in pair]

    out, sink, source = three_blocks(source_slice, pieces, tau, (got_n, got_b, got_c), spins)
    return last_block(sink, source, got_a, got_d, out)


def fits(mesh, eigenvectors, perambulator):
    n = eigenvectors.shape[4]
    space = mesh.shape["space"]
    return (
        eigenvectors.shape[0] == mesh.shape["cfg"] * mesh.shape["tm"]
        and space == SPINS
        and mesh.shape["tm"] == 4
        and perambulator.shape[2] == space * n
        and perambulator.shape[3] == space * n
        and eigenvectors.shape[3] % (128 * space) == 0
        and n % 128 == 0
    )


def solution(mesh):
    placed = (
        P(("cfg", "tm"), None, None, "space", None),
        P(("cfg", "tm"), None, None, "space"),
        P(),
        P(),
        P(),
    )

    def mapped(body):
        return jax.shard_map(
            body,
            mesh=mesh,
            in_specs=placed,
            out_specs=P(("cfg", "tm"), None, "space", None),
            check_vma=False,
        )

    def program(*arrays):
        if not fits(mesh, arrays[0], arrays[1]):
            return mapped(general_body)(*arrays)
        return mapped(block_body)(*arrays)

    return program
```

```python
import math

import jax
import jax.numpy as jnp
from jax import lax
from jax.experimental import pallas as pl
from jax.experimental.pallas import tpu as pltpu
from jax.sharding import PartitionSpec as P


LSIDE = 64
SPINS = 4


def spread(value, axis, source):
    kept = jnp.where(lax.axis_index(axis) == source, value, 0).astype(value.dtype)
    return lax.psum(kept, axis)


def site_phases(momenta, first_site, site_count):
    site_index = first_site + lax.iota(jnp.int32, site_count)
    along_x = site_index % LSIDE
    along_y = site_index // LSIDE % LSIDE
    along_z = site_index // (LSIDE * LSIDE)
    turn_count = (
        momenta[:, 0:1] * along_x[None, :]
        + momenta[:, 1:2] * along_y[None, :]
        + momenta[:, 2:3] * along_z[None, :]
    )
    phase_angle = (turn_count % LSIDE).astype(jnp.float32) * (2.0 * math.pi / LSIDE)
    return (jnp.cos(phase_angle), jnp.sin(phase_angle))


def split_elementals(product, vector_count):
    lead_shape = product.shape[:-2]
    product_grid = product.reshape(lead_shape + (2, vector_count, 2, 2, vector_count))
    real_part = product_grid[..., 0, :, :, 0, :] + product_grid[..., 1, :, :, 1, :]
    imaginary = product_grid[..., 0, :, :, 1, :] - product_grid[..., 1, :, :, 0, :]
    stacked = jnp.stack([real_part, imaginary], axis=-4)
    return jnp.moveaxis(stacked, -2, -4)


def elementals(vectors, cosine, sine_part):
    slab_count, color_count, site_count, vector_count = (
        vectors.shape[0],
        vectors.shape[2],
        vectors.shape[3],
        vectors.shape[4],
    )
    row_count = color_count * site_count
    real_rows = vectors[:, 0].reshape(slab_count, row_count, vector_count)
    imaginary_rows = vectors[:, 1].reshape(slab_count, row_count, vector_count)
    cos_rows = jnp.broadcast_to(cosine[:, None, :], (2, color_count, site_count)).reshape(
        1, 2, row_count, 1
    )
    sin_rows = jnp.broadcast_to(sine_part[:, None, :], (2, color_count, site_count)).reshape(
        1, 2, row_count, 1
    )
    phased_real = (cos_rows * real_rows[:, None] + sin_rows * imaginary_rows[:, None]).astype(
        jnp.bfloat16
    )
    phased_imaginary = (cos_rows * imaginary_rows[:, None] - sin_rows * real_rows[:, None]).astype(
        jnp.bfloat16
    )
    phased = jnp.concatenate([phased_real, phased_imaginary], axis=3)
    phased = jnp.transpose(phased, (0, 2, 1, 3)).reshape(slab_count, row_count, 4 * vector_count)
    plain_vectors = jnp.concatenate([real_rows, imaginary_rows], axis=2)
    product = lax.dot_general(
        plain_vectors, phased, (((1,), (1,)), ((0,), (0,))), preferred_element_type=jnp.float32
    )
    return split_elementals(product, vector_count)


def source_block(chosen):
    real_t = chosen[0].T
    imaginary_t = chosen[1].T
    upper = jnp.concatenate([real_t, -imaginary_t], axis=1)
    lower = jnp.concatenate([imaginary_t, real_t], axis=1)
    return jnp.concatenate([upper, lower], axis=0)


def propagate(sink_matrix, tau):
    vector_count = sink_matrix.shape[1]
    spin_count = tau.shape[1] // vector_count
    column_count = tau.shape[2]
    real_part, imaginary = (sink_matrix[0], sink_matrix[1])
    upper = jnp.concatenate([real_part, -imaginary], axis=1)
    lower = jnp.concatenate([imaginary, real_part], axis=1)
    sink_big = jnp.concatenate([upper, lower], axis=0)
    stacked = jnp.transpose(tau.reshape(2, spin_count, vector_count, column_count), (0, 2, 1, 3))
    stacked = stacked.reshape(2 * vector_count, spin_count * column_count)
    product = jnp.dot(sink_big, stacked, preferred_element_type=jnp.float32)
    product = jnp.transpose(
        product.reshape(2, vector_count, spin_count, column_count), (0, 2, 1, 3)
    )
    return product.reshape(2, spin_count * vector_count, column_count).astype(jnp.bfloat16)


def attach_source(propagated, source_big):
    vector_count = source_big.shape[0] // 2
    row_count = propagated.shape[1]
    spin_count = propagated.shape[2] // vector_count
    stacked = jnp.concatenate(
        [
            propagated[0].reshape(row_count, spin_count, vector_count),
            propagated[1].reshape(row_count, spin_count, vector_count),
        ],
        axis=2,
    )
    product = jnp.dot(
        stacked.reshape(row_count * spin_count, 2 * vector_count),
        source_big,
        preferred_element_type=jnp.float32,
    )
    product = jnp.transpose(product.reshape(row_count, spin_count, 2, vector_count), (2, 0, 1, 3))
    return product.reshape(2, row_count, spin_count * vector_count)


def general_body(eigenvectors, perambulator, momenta, ratios, source_slice):
    slab_count = eigenvectors.shape[0]
    color_count = eigenvectors.shape[2]
    site_count = eigenvectors.shape[3]
    vector_count = eigenvectors.shape[4]
    first_site = lax.axis_index("space") * site_count
    cosine, sine_part = site_phases(momenta, first_site, site_count)
    normalizer = 1.0 / math.sqrt(color_count * site_count * lax.axis_size("space") * vector_count)
    weights = (
        ratios[:, 0].astype(jnp.float32) / ratios[:, 1].astype(jnp.float32) * normalizer
    ).reshape(1, 2, 1, 1, 1)
    parts = elementals(eigenvectors, cosine, sine_part)
    partial_sums = jnp.sum(weights * parts, axis=1, keepdims=True)
    summed = lax.psum(partial_sums, "space")
    sink_matrices = summed[:, 0].astype(jnp.bfloat16)
    global_slice = source_slice[0] % (slab_count * lax.axis_size("tm"))
    local_source = lax.dynamic_index_in_dim(
        sink_matrices, global_slice % slab_count, 0, keepdims=False
    )
    chosen = spread(local_source, "tm", global_slice // slab_count)
    source_big = source_block(chosen)
    results = []
    for slab in range(slab_count):
        propagated = propagate(sink_matrices[slab], perambulator[slab])[None]
        turned = lax.all_to_all(propagated, "space", split_axis=2, concat_axis=3, tiled=True)
        results.append(attach_source(turned[0], source_big))
    return jnp.stack(results)


HBM = pl.BlockSpec(memory_space=pltpu.MemorySpace.HBM)


def in_hbm(array):
    return pltpu.with_memory_space_constraint(array, pltpu.MemorySpace.HBM)


def pick_kernel(tau_hbm, by3, by1, by2, buffer, in_sems, out_sems):
    place = lax.axis_index("space")
    loads = []
    stores = []
    for i, (r, out) in enumerate(((3, by3), (1, by1), (2, by2))):
        loads.append(pltpu.make_async_copy(tau_hbm.at[:, place ^ r], buffer.at[i], in_sems.at[i]))
        stores.append(pltpu.make_async_copy(buffer.at[i], out, out_sems.at[i]))
    for copy in loads:
        copy.start()
    for load, store in zip(loads, stores):
        load.wait()
        store.start()
    for copy in stores:
        copy.wait()


def pick_blocks(tau):
    _, _, n, columns = tau.shape
    return pl.pallas_call(
        pick_kernel,
        in_specs=[HBM],
        out_specs=[HBM] * 3,
        scratch_shapes=[
            pltpu.VMEM((3, 2, n, columns), tau.dtype),
            pltpu.SemaphoreType.DMA((3,)),
            pltpu.SemaphoreType.DMA((3,)),
        ],
        out_shape=[jax.ShapeDtypeStruct((2, n, columns), tau.dtype)] * 3,
        name="pick",
    )(in_hbm(tau))


def elemental_kernel(
    momenta_hbm,
    ratios_hbm,
    v_hbm,
    rounded_a,
    rounded_b,
    full_a,
    full_b,
    vectors,
    table,
    phased,
    total,
    momenta,
    ratios,
    sems,
    small_sems,
):
    place = lax.axis_index("space")
    colors = v_hbm.shape[1]
    site_count = v_hbm.shape[2]
    n = v_hbm.shape[3]
    half = n // 2
    loads = [
        pltpu.make_async_copy(v_hbm.at[:, c], vectors.at[c], sems.at[c]) for c in range(colors)
    ]
    small = [
        pltpu.make_async_copy(momenta_hbm, momenta, small_sems.at[0]),
        pltpu.make_async_copy(ratios_hbm, ratios, small_sems.at[1]),
    ]
    for copy in small + loads:
        copy.start()
    for copy in small:
        copy.wait()

    row = lax.broadcasted_iota(jnp.int32, (8, 128), 0)
    lane = lax.broadcasted_iota(jnp.int32, (8, 128), 1)
    second = (row & 1) == 1
    along = [jnp.where(second, momenta[1, a], momenta[0, a]) for a in range(3)]
    shift = jnp.where((row & 2) == 2, LSIDE - LSIDE // 4, 0)
    for tile in range(site_count // 128):
        site = place * site_count + tile * 128 + lane
        turn = (
            along[0] * (site % LSIDE)
            + along[1] * (site // LSIDE % LSIDE)
            + along[2] * (site // (LSIDE * LSIDE))
            + shift
        )
        turn = turn & (LSIDE - 1)
        angle = turn.astype(jnp.float32) * (2.0 * math.pi / LSIDE)
        table[pl.ds(tile * 128, 128), 0:8] = jnp.cos(angle).T

    def phase(color, k):
        slot = (2 * color + k) % 2
        real = vectors[color, 0].astype(jnp.float32)
        imag = vectors[color, 1].astype(jnp.float32)
        c = table[:, k : k + 1]
        s = table[:, k + 2 : k + 3]
        phased[slot, :, 0:n] = (c * real + s * imag).astype(jnp.bfloat16)
        phased[slot, :, n : 2 * n] = (c * imag - s * real).astype(jnp.bfloat16)

    def multiply(color, k):
        slot = (2 * color + k) % 2
        cols = slice(2 * k * n, (2 * k + 2) * n)
        for part in range(2):
            product = lax.dot_general(
                vectors[color, part],
                phased[slot],
                (((0,), (0,)), ((), ())),
                preferred_element_type=jnp.float32,
            )
            rows = slice(part * n, (part + 1) * n)
            if color == 0:
                total[rows, cols] = product
            else:
                total[rows, cols] += product

    before = None
    for color in range(colors):
        loads[color].wait()
        for k in range(2):
            phase(color, k)
            if before is not None:
                multiply(*before)
            before = (color, k)
    multiply(*before)

    normalizer = 1.0 / math.sqrt(colors * site_count * lax.axis_size("space") * n)
    re = 0.0
    im = 0.0
    for k in range(2):
        ratio = [jnp.full((8, 128), ratios[k, i], jnp.int32).astype(jnp.float32) for i in range(2)]
        w = (ratio[0] / ratio[1] * normalizer)[0:1, 0:1]
        zr = slice((2 * k) * n, (2 * k + 1) * n)
        zi = slice((2 * k + 1) * n, (2 * k + 2) * n)
        re += w * (total[0:n, zr] + total[n : 2 * n, zi])
        im += w * (total[0:n, zi] - total[n : 2 * n, zr])
    for part, value in enumerate((re, im)):
        small = value.astype(jnp.bfloat16)
        rounded_a[part] = small[:half]
        rounded_b[part] = small[half:]
        full_a[part] = value[:half]
        full_b[part] = value[half:]


def elemental_sums(vectors, momenta, ratios):
    _, color_count, site_count, n = vectors.shape
    half = n // 2
    rows = pl.BlockSpec((2, half, n), lambda i: (0, 0, 0))
    return pl.pallas_call(
        elemental_kernel,
        grid=(1,),
        in_specs=[HBM] * 3,
        out_specs=[rows] * 4,
        scratch_shapes=[
                pltpu.VMEM((color_count, 2, site_count, n), jnp.bfloat16),
                pltpu.VMEM((site_count, 128), jnp.float32),
                pltpu.VMEM((2, site_count, 2 * n), jnp.bfloat16),
                pltpu.VMEM((2 * n, 4 * n), jnp.float32),
                pltpu.SMEM(momenta.shape, jnp.int32),
                pltpu.SMEM(ratios.shape, jnp.int32),
                pltpu.SemaphoreType.DMA((color_count,)),
                pltpu.SemaphoreType.DMA((2,)),
        ],
        out_shape=[
            jax.ShapeDtypeStruct((2, half, n), dtype)
            for dtype in (jnp.bfloat16, jnp.bfloat16, jnp.float32, jnp.float32)
        ],
        compiler_params=pltpu.CompilerParams(vmem_limit_bytes=40 * 1024 * 1024),
        name="elementals",
    )(in_hbm(momenta), in_hbm(ratios), in_hbm(vectors))


def complex_rows(real, imag):
    upper = jnp.concatenate([real, imag], axis=1)
    lower = jnp.concatenate([-imag, real], axis=1)
    return jnp.concatenate([upper, lower], axis=0)


def sandwich(sink, tau_re, tau_im, source):
    prop = jnp.dot(sink, complex_rows(tau_re, tau_im), preferred_element_type=jnp.float32)
    return lax.dot_general(
        prop.astype(jnp.bfloat16),
        source,
        (((1,), (1,)), ((), ())),
        preferred_element_type=jnp.float32,
    )


def copy_if(flag, first, second, target, sem):
    @pl.when(flag == 1)
    def _():
        pltpu.make_async_copy(first, target, sem).start()

    @pl.when(flag != 1)
    def _():
        pltpu.make_async_copy(second, target, sem).start()


def is_inner(place):
    return jnp.where((place == 1) | (place == 2), 1, 0)


def three_kernel(source_slice, *refs):
    (sink_a, sink_b, here_a, here_b, far_a, far_b, beside_a, beside_b) = refs[:8]
    tau_hbm, got_n, got_a, got_c = refs[8:12]
    out_hbm, sink_out, source_out = refs[12:15]
    blocks, staged, block_sems, out_sems = refs[15:]
    n = sink_out.shape[0]
    place = lax.axis_index("space")
    time = lax.axis_index("tm")
    inner = is_inner(place)
    same = jnp.where(source_slice[0] % lax.axis_size("tm") // 2 == time // 2, 1, 0)
    odd = time % 2

    pltpu.make_async_copy(tau_hbm.at[:, place], blocks.at[0], block_sems.at[0]).start()
    pltpu.make_async_copy(got_n, blocks.at[1], block_sems.at[1]).start()
    copy_if(inner, got_a, got_c, blocks.at[2], block_sems.at[2])

    def halves(first, second):
        return jnp.concatenate([first, second], axis=0)

    sink = [halves(sink_a[part], sink_b[part]) for part in range(2)]
    sink_rows = jnp.concatenate(sink, axis=1)
    sink_out[...] = sink_rows

    def away(far, beside, part):
        upper = jnp.where(odd == 0, far[part], beside[part])
        lower = jnp.where(odd == 0, beside[part], far[part])
        return halves(upper, lower)

    source = [
        halves(
            *[
                jnp.where(same == 1, here[part], away(far, beside, part))
                for here, far, beside in ((here_a, far_a, beside_a), (here_b, far_b, beside_b))
            ]
        )
        for part in range(2)
    ]
    source_rows = complex_rows(*source)
    source_out[...] = source_rows

    stores = []
    for i in range(3):
        pltpu.make_async_copy(got_n, blocks.at[i], block_sems.at[i]).wait()
        product = sandwich(sink_rows, blocks[i, 0], blocks[i, 1], source_rows)
        staged[i, 0] = product[:, :n]
        staged[i, 1] = product[:, n:]
        partner = place ^ (i if i < 2 else 2 + inner)
        column = pl.multiple_of(partner * n, 128)
        store = pltpu.make_async_copy(
            staged.at[i], out_hbm.at[0, :, :, pl.ds(column, n)], out_sems.at[i]
        )
        store.start()
        stores.append(store)
    for store in stores:
        store.wait()


def three_blocks(source_slice, pieces, tau, got, spins):
    n = tau.shape[2]
    return pl.pallas_call(
        three_kernel,
        grid_spec=pltpu.PrefetchScalarGridSpec(
            num_scalar_prefetch=1,
            grid=(1,),
            in_specs=[pl.BlockSpec(piece.shape, lambda i, *_: (0, 0, 0)) for piece in pieces]
            + [HBM] * 4,
            out_specs=[
                HBM,
                pl.BlockSpec((n, 2 * n), lambda i, *_: (0, 0)),
                pl.BlockSpec((2 * n, 2 * n), lambda i, *_: (0, 0)),
            ],
            scratch_shapes=[
                pltpu.VMEM((3, 2, n, n), jnp.bfloat16),
                pltpu.VMEM((3, 2, n, n), jnp.float32),
                pltpu.SemaphoreType.DMA((3,)),
                pltpu.SemaphoreType.DMA((3,)),
            ],
        ),
        out_shape=[
            jax.ShapeDtypeStruct((1, 2, n, spins * n), jnp.float32),
            jax.ShapeDtypeStruct((n, 2 * n), jnp.bfloat16),
            jax.ShapeDtypeStruct((2 * n, 2 * n), jnp.bfloat16),
        ],
        compiler_params=pltpu.CompilerParams(vmem_limit_bytes=40 * 1024 * 1024),
        name="three",
    )(source_slice, *pieces, tau, *got)


def last_kernel(sink, source, got_b, got_d, _, out_hbm, block, staged, sem, out_sem):
    n = sink.shape[0]
    place = lax.axis_index("space")
    inner = is_inner(place)
    copy_if(inner, got_b, got_d, block, sem)
    pltpu.make_async_copy(got_b, block, sem).wait()
    product = sandwich(sink[...], block[0], block[1], source[...])
    staged[0] = product[:, :n]
    staged[1] = product[:, n:]
    column = pl.multiple_of((place ^ (3 - inner)) * n, 128)
    store = pltpu.make_async_copy(staged, out_hbm.at[0, :, :, pl.ds(column, n)], out_sem)
    store.start()
    store.wait()


def last_block(sink, source, got_b, got_d, out):
    n = sink.shape[0]
    return pl.pallas_call(
        last_kernel,
        grid=(1,),
        in_specs=[
            pl.BlockSpec((n, 2 * n), lambda i: (0, 0)),
            pl.BlockSpec((2 * n, 2 * n), lambda i: (0, 0)),
            HBM,
            HBM,
            HBM,
        ],
        out_specs=HBM,
        scratch_shapes=[
            pltpu.VMEM((2, n, n), jnp.bfloat16),
            pltpu.VMEM((2, n, n), jnp.float32),
            pltpu.SemaphoreType.DMA,
            pltpu.SemaphoreType.DMA,
        ],
        out_shape=jax.ShapeDtypeStruct(out.shape, out.dtype),
        input_output_aliases={4: 0},
        compiler_params=pltpu.CompilerParams(vmem_limit_bytes=40 * 1024 * 1024),
        name="last",
    )(sink, source, got_b, got_d, out)


def block_body(eigenvectors, perambulator, momenta, ratios, source_slice):
    return ordered_body(eigenvectors, perambulator, momenta, ratios, source_slice)


def ordered_body(eigenvectors, perambulator, momenta, ratios, source_slice):
    n = eigenvectors.shape[4]
    quarter = n // 4
    spins = lax.axis_size("space")
    j = lax.axis_index("space")
    inner = (j == 1) | (j == 2)
    odd = lax.axis_index("tm") % 2
    tau = perambulator[0].reshape(2, spins, n, n)

    def move(value, pairs, axis="space"):
        return lax.ppermute(value, axis, pairs)

    middle = [(1, 2), (2, 1)]
    ends = [(0, 3), (3, 0)]
    inward = [(0, 1), (3, 2)]
    outward = [(1, 0), (2, 3)]
    skip_in = [(0, 2), (3, 1)]
    skip_out = [(1, 3), (2, 0)]
    core = [(0, 1), (1, 0), (2, 3), (3, 2)]
    chip = [(0, 2), (2, 0), (1, 3), (3, 1)]

    by3, by1, by2 = pick_blocks(tau)
    got_a = move(by3, middle)
    got_n = move(by1, inward + outward)
    got_c = move(by2, skip_out)
    rounded_a, rounded_b, full_a, full_b = elemental_sums(eigenvectors[0], momenta, ratios)
    got_b = move(by2, skip_in)
    got_d = move(by3, ends)

    pieces = []
    for rounded, full in ((rounded_a, full_a), (rounded_b, full_b)):
        inside = move(rounded, inward)
        pair = full + inside.astype(jnp.float32)
        across = move(pair.astype(jnp.bfloat16), middle)
        summed = (pair + across.astype(jnp.float32)).astype(jnp.bfloat16)
        outside = move(summed, outward)
        sink = jnp.where(inner, summed, outside)
        partner = move(sink, core, "tm")
        here = jnp.where(source_slice[0] % 2 == odd, sink, partner)
        mine = lax.dynamic_slice_in_dim(here, odd * quarter, quarter, 1)
        far = move(mine, chip, "tm")
        beside = move(far, core, "tm")
        pieces.append((sink, here, far, beside))
    pieces = [piece for pair in zip(*pieces) for piece in pair]

    out, sink, source = three_blocks(source_slice, pieces, tau, (got_n, got_a, got_c), spins)
    return last_block(sink, source, got_b, got_d, out)


def fits(mesh, eigenvectors, perambulator):
    n = eigenvectors.shape[4]
    space = mesh.shape["space"]
    return (
        eigenvectors.shape[0] == mesh.shape["cfg"] * mesh.shape["tm"]
        and space == SPINS
        and mesh.shape["tm"] == 4
        and perambulator.shape[2] == space * n
        and perambulator.shape[3] == space * n
        and eigenvectors.shape[3] % (128 * space) == 0
        and n % 128 == 0
    )


def solution(mesh):
    placed = (
        P(("cfg", "tm"), None, None, "space", None),
        P(("cfg", "tm"), None, None, "space"),
        P(),
        P(),
        P(),
    )

    def mapped(body):
        return jax.shard_map(
            body,
            mesh=mesh,
            in_specs=placed,
            out_specs=P(("cfg", "tm"), None, "space", None),
            check_vma=False,
        )

    def program(*arrays):
        if not fits(mesh, arrays[0], arrays[1]):
            return mapped(general_body)(*arrays)
        return mapped(block_body)(*arrays)

    return program
```

```python
import math

import jax
import jax.numpy as jnp
from jax import lax
from jax.experimental import pallas as pl
from jax.experimental.pallas import tpu as pltpu
from jax.sharding import PartitionSpec as P


LSIDE = 64
SPINS = 4


def spread(value, axis, source):
    kept = jnp.where(lax.axis_index(axis) == source, value, 0).astype(value.dtype)
    return lax.psum(kept, axis)


def site_phases(momenta, first_site, site_count):
    site_index = first_site + lax.iota(jnp.int32, site_count)
    along_x = site_index % LSIDE
    along_y = site_index // LSIDE % LSIDE
    along_z = site_index // (LSIDE * LSIDE)
    turn_count = (
        momenta[:, 0:1] * along_x[None, :]
        + momenta[:, 1:2] * along_y[None, :]
        + momenta[:, 2:3] * along_z[None, :]
    )
    phase_angle = (turn_count % LSIDE).astype(jnp.float32) * (2.0 * math.pi / LSIDE)
    return (jnp.cos(phase_angle), jnp.sin(phase_angle))


def split_elementals(product, vector_count):
    lead_shape = product.shape[:-2]
    product_grid = product.reshape(lead_shape + (2, vector_count, 2, 2, vector_count))
    real_part = product_grid[..., 0, :, :, 0, :] + product_grid[..., 1, :, :, 1, :]
    imaginary = product_grid[..., 0, :, :, 1, :] - product_grid[..., 1, :, :, 0, :]
    stacked = jnp.stack([real_part, imaginary], axis=-4)
    return jnp.moveaxis(stacked, -2, -4)


def elementals(vectors, cosine, sine_part):
    slab_count, color_count, site_count, vector_count = (
        vectors.shape[0],
        vectors.shape[2],
        vectors.shape[3],
        vectors.shape[4],
    )
    row_count = color_count * site_count
    real_rows = vectors[:, 0].reshape(slab_count, row_count, vector_count)
    imaginary_rows = vectors[:, 1].reshape(slab_count, row_count, vector_count)
    cos_rows = jnp.broadcast_to(cosine[:, None, :], (2, color_count, site_count)).reshape(
        1, 2, row_count, 1
    )
    sin_rows = jnp.broadcast_to(sine_part[:, None, :], (2, color_count, site_count)).reshape(
        1, 2, row_count, 1
    )
    phased_real = (cos_rows * real_rows[:, None] + sin_rows * imaginary_rows[:, None]).astype(
        jnp.bfloat16
    )
    phased_imaginary = (cos_rows * imaginary_rows[:, None] - sin_rows * real_rows[:, None]).astype(
        jnp.bfloat16
    )
    phased = jnp.concatenate([phased_real, phased_imaginary], axis=3)
    phased = jnp.transpose(phased, (0, 2, 1, 3)).reshape(slab_count, row_count, 4 * vector_count)
    plain_vectors = jnp.concatenate([real_rows, imaginary_rows], axis=2)
    product = lax.dot_general(
        plain_vectors, phased, (((1,), (1,)), ((0,), (0,))), preferred_element_type=jnp.float32
    )
    return split_elementals(product, vector_count)


def source_block(chosen):
    real_t = chosen[0].T
    imaginary_t = chosen[1].T
    upper = jnp.concatenate([real_t, -imaginary_t], axis=1)
    lower = jnp.concatenate([imaginary_t, real_t], axis=1)
    return jnp.concatenate([upper, lower], axis=0)


def propagate(sink_matrix, tau):
    vector_count = sink_matrix.shape[1]
    spin_count = tau.shape[1] // vector_count
    column_count = tau.shape[2]
    real_part, imaginary = (sink_matrix[0], sink_matrix[1])
    upper = jnp.concatenate([real_part, -imaginary], axis=1)
    lower = jnp.concatenate([imaginary, real_part], axis=1)
    sink_big = jnp.concatenate([upper, lower], axis=0)
    stacked = jnp.transpose(tau.reshape(2, spin_count, vector_count, column_count), (0, 2, 1, 3))
    stacked = stacked.reshape(2 * vector_count, spin_count * column_count)
    product = jnp.dot(sink_big, stacked, preferred_element_type=jnp.float32)
    product = jnp.transpose(
        product.reshape(2, vector_count, spin_count, column_count), (0, 2, 1, 3)
    )
    return product.reshape(2, spin_count * vector_count, column_count).astype(jnp.bfloat16)


def attach_source(propagated, source_big):
    vector_count = source_big.shape[0] // 2
    row_count = propagated.shape[1]
    spin_count = propagated.shape[2] // vector_count
    stacked = jnp.concatenate(
        [
            propagated[0].reshape(row_count, spin_count, vector_count),
            propagated[1].reshape(row_count, spin_count, vector_count),
        ],
        axis=2,
    )
    product = jnp.dot(
        stacked.reshape(row_count * spin_count, 2 * vector_count),
        source_big,
        preferred_element_type=jnp.float32,
    )
    product = jnp.transpose(product.reshape(row_count, spin_count, 2, vector_count), (2, 0, 1, 3))
    return product.reshape(2, row_count, spin_count * vector_count)


def general_body(eigenvectors, perambulator, momenta, ratios, source_slice):
    slab_count = eigenvectors.shape[0]
    color_count = eigenvectors.shape[2]
    site_count = eigenvectors.shape[3]
    vector_count = eigenvectors.shape[4]
    first_site = lax.axis_index("space") * site_count
    cosine, sine_part = site_phases(momenta, first_site, site_count)
    normalizer = 1.0 / math.sqrt(color_count * site_count * lax.axis_size("space") * vector_count)
    weights = (
        ratios[:, 0].astype(jnp.float32) / ratios[:, 1].astype(jnp.float32) * normalizer
    ).reshape(1, 2, 1, 1, 1)
    parts = elementals(eigenvectors, cosine, sine_part)
    partial_sums = jnp.sum(weights * parts, axis=1, keepdims=True)
    summed = lax.psum(partial_sums, "space")
    sink_matrices = summed[:, 0].astype(jnp.bfloat16)
    global_slice = source_slice[0] % (slab_count * lax.axis_size("tm"))
    local_source = lax.dynamic_index_in_dim(
        sink_matrices, global_slice % slab_count, 0, keepdims=False
    )
    chosen = spread(local_source, "tm", global_slice // slab_count)
    source_big = source_block(chosen)
    results = []
    for slab in range(slab_count):
        propagated = propagate(sink_matrices[slab], perambulator[slab])[None]
        turned = lax.all_to_all(propagated, "space", split_axis=2, concat_axis=3, tiled=True)
        results.append(attach_source(turned[0], source_big))
    return jnp.stack(results)


HBM = pl.BlockSpec(memory_space=pltpu.MemorySpace.HBM)


def in_hbm(array):
    return pltpu.with_memory_space_constraint(array, pltpu.MemorySpace.HBM)


def pick_kernel(tau_hbm, by3, by1, by2, buffer, in_sems, out_sems):
    place = lax.axis_index("space")
    loads = []
    stores = []
    for i, (r, out) in enumerate(((3, by3), (1, by1), (2, by2))):
        loads.append(pltpu.make_async_copy(tau_hbm.at[:, place ^ r], buffer.at[i], in_sems.at[i]))
        stores.append(pltpu.make_async_copy(buffer.at[i], out, out_sems.at[i]))
    for copy in loads:
        copy.start()
    for load, store in zip(loads, stores):
        load.wait()
        store.start()
    for copy in stores:
        copy.wait()


def pick_blocks(tau):
    _, _, n, columns = tau.shape
    return pl.pallas_call(
        pick_kernel,
        in_specs=[HBM],
        out_specs=[HBM] * 3,
        scratch_shapes=[
            pltpu.VMEM((3, 2, n, columns), tau.dtype),
            pltpu.SemaphoreType.DMA((3,)),
            pltpu.SemaphoreType.DMA((3,)),
        ],
        out_shape=[jax.ShapeDtypeStruct((2, n, columns), tau.dtype)] * 3,
        name="pick",
    )(in_hbm(tau))


def elemental_kernel(
    momenta_hbm,
    ratios_hbm,
    v_hbm,
    rounded_a,
    rounded_b,
    full_a,
    full_b,
    vectors,
    table,
    phased,
    total,
    momenta,
    ratios,
    sems,
    small_sems,
):
    place = lax.axis_index("space")
    colors = v_hbm.shape[1]
    site_count = v_hbm.shape[2]
    n = v_hbm.shape[3]
    half = n // 2
    loads = [
        pltpu.make_async_copy(v_hbm.at[:, c], vectors.at[c], sems.at[c]) for c in range(colors)
    ]
    small = [
        pltpu.make_async_copy(momenta_hbm, momenta, small_sems.at[0]),
        pltpu.make_async_copy(ratios_hbm, ratios, small_sems.at[1]),
    ]
    for copy in small + loads:
        copy.start()
    for copy in small:
        copy.wait()

    row = lax.broadcasted_iota(jnp.int32, (8, 128), 0)
    lane = lax.broadcasted_iota(jnp.int32, (8, 128), 1)
    second = (row & 1) == 1
    along = [jnp.where(second, momenta[1, a], momenta[0, a]) for a in range(3)]
    shift = jnp.where((row & 2) == 2, LSIDE - LSIDE // 4, 0)
    for tile in range(site_count // 128):
        site = place * site_count + tile * 128 + lane
        turn = (
            along[0] * (site % LSIDE)
            + along[1] * (site // LSIDE % LSIDE)
            + along[2] * (site // (LSIDE * LSIDE))
            + shift
        )
        turn = turn & (LSIDE - 1)
        angle = turn.astype(jnp.float32) * (2.0 * math.pi / LSIDE)
        table[pl.ds(tile * 128, 128), 0:8] = jnp.cos(angle).T

    def phase(color, k):
        slot = (2 * color + k) % 2
        real = vectors[color, 0].astype(jnp.float32)
        imag = vectors[color, 1].astype(jnp.float32)
        c = table[:, k : k + 1]
        s = table[:, k + 2 : k + 3]
        phased[slot, :, 0:n] = (c * real + s * imag).astype(jnp.bfloat16)
        phased[slot, :, n : 2 * n] = (c * imag - s * real).astype(jnp.bfloat16)

    def multiply(color, k):
        slot = (2 * color + k) % 2
        cols = slice(2 * k * n, (2 * k + 2) * n)
        for part in range(2):
            product = lax.dot_general(
                vectors[color, part],
                phased[slot],
                (((0,), (0,)), ((), ())),
                preferred_element_type=jnp.float32,
            )
            rows = slice(part * n, (part + 1) * n)
            if color == 0:
                total[rows, cols] = product
            else:
                total[rows, cols] += product

    before = None
    for color in range(colors):
        loads[color].wait()
        for k in range(2):
            phase(color, k)
            if before is not None:
                multiply(*before)
            before = (color, k)
    multiply(*before)

    normalizer = 1.0 / math.sqrt(colors * site_count * lax.axis_size("space") * n)
    re = 0.0
    im = 0.0
    for k in range(2):
        ratio = [jnp.full((8, 128), ratios[k, i], jnp.int32).astype(jnp.float32) for i in range(2)]
        w = (ratio[0] / ratio[1] * normalizer)[0:1, 0:1]
        zr = slice((2 * k) * n, (2 * k + 1) * n)
        zi = slice((2 * k + 1) * n, (2 * k + 2) * n)
        re += w * (total[0:n, zr] + total[n : 2 * n, zi])
        im += w * (total[0:n, zi] - total[n : 2 * n, zr])
    for part, value in enumerate((re, im)):
        small = value.astype(jnp.bfloat16)
        rounded_a[part] = small[:half]
        rounded_b[part] = small[half:]
        full_a[part] = value[:half]
        full_b[part] = value[half:]


def elemental_sums(vectors, momenta, ratios):
    _, color_count, site_count, n = vectors.shape
    half = n // 2
    rows = pl.BlockSpec((2, half, n), lambda i: (0, 0, 0))
    return pl.pallas_call(
        elemental_kernel,
        grid=(1,),
        in_specs=[HBM] * 3,
        out_specs=[rows] * 4,
        scratch_shapes=[
                pltpu.VMEM((color_count, 2, site_count, n), jnp.bfloat16),
                pltpu.VMEM((site_count, 128), jnp.float32),
                pltpu.VMEM((2, site_count, 2 * n), jnp.bfloat16),
                pltpu.VMEM((2 * n, 4 * n), jnp.float32),
                pltpu.SMEM(momenta.shape, jnp.int32),
                pltpu.SMEM(ratios.shape, jnp.int32),
                pltpu.SemaphoreType.DMA((color_count,)),
                pltpu.SemaphoreType.DMA((2,)),
        ],
        out_shape=[
            jax.ShapeDtypeStruct((2, half, n), dtype)
            for dtype in (jnp.bfloat16, jnp.bfloat16, jnp.float32, jnp.float32)
        ],
        compiler_params=pltpu.CompilerParams(vmem_limit_bytes=40 * 1024 * 1024),
        name="elementals",
    )(in_hbm(momenta), in_hbm(ratios), in_hbm(vectors))


def complex_rows(real, imag):
    upper = jnp.concatenate([real, imag], axis=1)
    lower = jnp.concatenate([-imag, real], axis=1)
    return jnp.concatenate([upper, lower], axis=0)


def sandwich(sink, tau_re, tau_im, source):
    prop = jnp.dot(sink, complex_rows(tau_re, tau_im), preferred_element_type=jnp.float32)
    return lax.dot_general(
        prop.astype(jnp.bfloat16),
        source,
        (((1,), (1,)), ((), ())),
        preferred_element_type=jnp.float32,
    )


def three_kernel(source_slice, *refs):
    (sink_a, sink_b, here_a, here_b, far_a, far_b, beside_a, beside_b) = refs[:8]
    tau_hbm, got1, got3 = refs[8:11]
    out_hbm, sink_out, source_out = refs[11:14]
    blocks, staged, block_sems, out_sems = refs[14:]
    n = sink_out.shape[0]
    place = lax.axis_index("space")
    time = lax.axis_index("tm")
    same = jnp.where(source_slice[0] % lax.axis_size("tm") // 2 == time // 2, 1, 0)
    odd = time % 2

    pltpu.make_async_copy(tau_hbm.at[:, place], blocks.at[0], block_sems.at[0]).start()
    pltpu.make_async_copy(got1, blocks.at[1], block_sems.at[1]).start()
    pltpu.make_async_copy(got3, blocks.at[2], block_sems.at[2]).start()

    def halves(first, second):
        return jnp.concatenate([first, second], axis=0)

    sink = [halves(sink_a[part], sink_b[part]) for part in range(2)]
    sink_rows = jnp.concatenate(sink, axis=1)
    sink_out[...] = sink_rows

    def away(far, beside, part):
        upper = jnp.where(odd == 0, far[part], beside[part])
        lower = jnp.where(odd == 0, beside[part], far[part])
        return halves(upper, lower)

    source = [
        halves(
            *[
                jnp.where(same == 1, here[part], away(far, beside, part))
                for here, far, beside in ((here_a, far_a, beside_a), (here_b, far_b, beside_b))
            ]
        )
        for part in range(2)
    ]
    source_rows = complex_rows(*source)
    source_out[...] = source_rows

    stores = []
    for i in range(3):
        pltpu.make_async_copy(got1, blocks.at[i], block_sems.at[i]).wait()
        product = sandwich(sink_rows, blocks[i, 0], blocks[i, 1], source_rows)
        staged[i, 0] = product[:, :n]
        staged[i, 1] = product[:, n:]
        column = pl.multiple_of((place ^ (0, 1, 3)[i]) * n, 128)
        store = pltpu.make_async_copy(
            staged.at[i], out_hbm.at[0, :, :, pl.ds(column, n)], out_sems.at[i]
        )
        store.start()
        stores.append(store)
    for store in stores:
        store.wait()


def three_blocks(source_slice, pieces, tau, got, spins):
    n = tau.shape[2]
    return pl.pallas_call(
        three_kernel,
        grid_spec=pltpu.PrefetchScalarGridSpec(
            num_scalar_prefetch=1,
            grid=(1,),
            in_specs=[pl.BlockSpec(piece.shape, lambda i, *_: (0, 0, 0)) for piece in pieces]
            + [HBM] * 3,
            out_specs=[
                HBM,
                pl.BlockSpec((n, 2 * n), lambda i, *_: (0, 0)),
                pl.BlockSpec((2 * n, 2 * n), lambda i, *_: (0, 0)),
            ],
            scratch_shapes=[
                pltpu.VMEM((3, 2, n, n), jnp.bfloat16),
                pltpu.VMEM((3, 2, n, n), jnp.float32),
                pltpu.SemaphoreType.DMA((3,)),
                pltpu.SemaphoreType.DMA((3,)),
            ],
        ),
        out_shape=[
            jax.ShapeDtypeStruct((1, 2, n, spins * n), jnp.float32),
            jax.ShapeDtypeStruct((n, 2 * n), jnp.bfloat16),
            jax.ShapeDtypeStruct((2 * n, 2 * n), jnp.bfloat16),
        ],
        compiler_params=pltpu.CompilerParams(vmem_limit_bytes=40 * 1024 * 1024),
        name="three",
    )(source_slice, *pieces, tau, *got)


def last_kernel(sink, source, got2, _, out_hbm, block, staged, sem, out_sem):
    n = sink.shape[0]
    place = lax.axis_index("space")
    load = pltpu.make_async_copy(got2, block, sem)
    load.start()
    load.wait()
    product = sandwich(sink[...], block[0], block[1], source[...])
    staged[0] = product[:, :n]
    staged[1] = product[:, n:]
    column = pl.multiple_of((place ^ 2) * n, 128)
    store = pltpu.make_async_copy(staged, out_hbm.at[0, :, :, pl.ds(column, n)], out_sem)
    store.start()
    store.wait()


def last_block(sink, source, got2, out):
    n = sink.shape[0]
    return pl.pallas_call(
        last_kernel,
        grid=(1,),
        in_specs=[
            pl.BlockSpec((n, 2 * n), lambda i: (0, 0)),
            pl.BlockSpec((2 * n, 2 * n), lambda i: (0, 0)),
            HBM,
            HBM,
        ],
        out_specs=HBM,
        scratch_shapes=[
            pltpu.VMEM((2, n, n), jnp.bfloat16),
            pltpu.VMEM((2, n, n), jnp.float32),
            pltpu.SemaphoreType.DMA,
            pltpu.SemaphoreType.DMA,
        ],
        out_shape=jax.ShapeDtypeStruct(out.shape, out.dtype),
        input_output_aliases={3: 0},
        compiler_params=pltpu.CompilerParams(vmem_limit_bytes=40 * 1024 * 1024),
        name="last",
    )(sink, source, got2, out)


def xor_pairs(count, bit):
    return [(i, i ^ bit) for i in range(count)]


def block_body(eigenvectors, perambulator, momenta, ratios, source_slice):
    return ordered_body(eigenvectors, perambulator, momenta, ratios, source_slice)


def ordered_body(eigenvectors, perambulator, momenta, ratios, source_slice):
    n = eigenvectors.shape[4]
    quarter = n // 4
    spins = lax.axis_size("space")
    times = lax.axis_size("tm")
    j = lax.axis_index("space")
    inner = (j == 1) | (j == 2)
    odd = lax.axis_index("tm") % 2
    tau = perambulator[0].reshape(2, spins, n, n)

    def move(value, pairs, axis="space"):
        return lax.ppermute(value, axis, pairs)

    middle = [(1, 2), (2, 1)]
    inward = [(0, 1), (3, 2)]
    outward = [(1, 0), (2, 3)]
    core = xor_pairs(times, 1)
    chip = xor_pairs(times, 2)

    by3, by1, by2 = pick_blocks(tau)
    got3 = move(by3, xor_pairs(spins, 3))
    got1 = move(by1, xor_pairs(spins, 1))
    got2 = move(by2, xor_pairs(spins, 2))
    rounded_a, rounded_b, full_a, full_b = elemental_sums(eigenvectors[0], momenta, ratios)

    pieces = []
    for rounded, full in ((rounded_a, full_a), (rounded_b, full_b)):
        inside = move(rounded, inward)
        pair = full + inside.astype(jnp.float32)
        across = move(pair.astype(jnp.bfloat16), middle)
        summed = (pair + across.astype(jnp.float32)).astype(jnp.bfloat16)
        outside = move(summed, outward)
        sink = jnp.where(inner, summed, outside)
        partner = move(sink, core, "tm")
        here = jnp.where(source_slice[0] % 2 == odd, sink, partner)
        mine = lax.dynamic_slice_in_dim(here, odd * quarter, quarter, 1)
        far = move(mine, chip, "tm")
        beside = move(far, core, "tm")
        pieces.append((sink, here, far, beside))
    pieces = [piece for pair in zip(*pieces) for piece in pair]

    out, sink, source = three_blocks(source_slice, pieces, tau, [in_hbm(got) for got in (got1, got3)], spins)
    return last_block(sink, source, got2, out)


def fits(mesh, eigenvectors, perambulator):
    n = eigenvectors.shape[4]
    space = mesh.shape["space"]
    return (
        eigenvectors.shape[0] == mesh.shape["cfg"] * mesh.shape["tm"]
        and space == SPINS
        and mesh.shape["tm"] == 4
        and perambulator.shape[2] == space * n
        and perambulator.shape[3] == space * n
        and eigenvectors.shape[3] % (128 * space) == 0
        and n % 128 == 0
    )


def solution(mesh):
    placed = (
        P(("cfg", "tm"), None, None, "space", None),
        P(("cfg", "tm"), None, None, "space"),
        P(),
        P(),
        P(),
    )

    def mapped(body):
        return jax.shard_map(
            body,
            mesh=mesh,
            in_specs=placed,
            out_specs=P(("cfg", "tm"), None, "space", None),
            check_vma=False,
        )

    def program(*arrays):
        if not fits(mesh, arrays[0], arrays[1]):
            return mapped(general_body)(*arrays)
        return mapped(block_body)(*arrays)

    return program
```

```python
import functools
import math

import jax
import jax.numpy as jnp
from jax import lax
from jax.experimental import pallas as pl
from jax.experimental.pallas import tpu as pltpu
from jax.sharding import PartitionSpec as P


LSIDE = 64
SPINS = 4
PIECES = 2


def spread(value, axis, source):
    kept = jnp.where(lax.axis_index(axis) == source, value, 0).astype(value.dtype)
    return lax.psum(kept, axis)


def site_phases(momenta, first_site, site_count):
    site_index = first_site + lax.iota(jnp.int32, site_count)
    along_x = site_index % LSIDE
    along_y = site_index // LSIDE % LSIDE
    along_z = site_index // (LSIDE * LSIDE)
    turn_count = (
        momenta[:, 0:1] * along_x[None, :]
        + momenta[:, 1:2] * along_y[None, :]
        + momenta[:, 2:3] * along_z[None, :]
    )
    phase_angle = (turn_count % LSIDE).astype(jnp.float32) * (2.0 * math.pi / LSIDE)
    return (jnp.cos(phase_angle), jnp.sin(phase_angle))


def split_elementals(product, vector_count):
    lead_shape = product.shape[:-2]
    product_grid = product.reshape(lead_shape + (2, vector_count, 2, 2, vector_count))
    real_part = product_grid[..., 0, :, :, 0, :] + product_grid[..., 1, :, :, 1, :]
    imaginary = product_grid[..., 0, :, :, 1, :] - product_grid[..., 1, :, :, 0, :]
    stacked = jnp.stack([real_part, imaginary], axis=-4)
    return jnp.moveaxis(stacked, -2, -4)


def elementals(vectors, cosine, sine_part):
    slab_count, color_count, site_count, vector_count = (
        vectors.shape[0],
        vectors.shape[2],
        vectors.shape[3],
        vectors.shape[4],
    )
    row_count = color_count * site_count
    real_rows = vectors[:, 0].reshape(slab_count, row_count, vector_count)
    imaginary_rows = vectors[:, 1].reshape(slab_count, row_count, vector_count)
    cos_rows = jnp.broadcast_to(cosine[:, None, :], (2, color_count, site_count)).reshape(
        1, 2, row_count, 1
    )
    sin_rows = jnp.broadcast_to(sine_part[:, None, :], (2, color_count, site_count)).reshape(
        1, 2, row_count, 1
    )
    phased_real = (cos_rows * real_rows[:, None] + sin_rows * imaginary_rows[:, None]).astype(
        jnp.bfloat16
    )
    phased_imaginary = (cos_rows * imaginary_rows[:, None] - sin_rows * real_rows[:, None]).astype(
        jnp.bfloat16
    )
    phased = jnp.concatenate([phased_real, phased_imaginary], axis=3)
    phased = jnp.transpose(phased, (0, 2, 1, 3)).reshape(slab_count, row_count, 4 * vector_count)
    plain_vectors = jnp.concatenate([real_rows, imaginary_rows], axis=2)
    product = lax.dot_general(
        plain_vectors, phased, (((1,), (1,)), ((0,), (0,))), preferred_element_type=jnp.float32
    )
    return split_elementals(product, vector_count)


def source_block(chosen):
    real_t = chosen[0].T
    imaginary_t = chosen[1].T
    upper = jnp.concatenate([real_t, -imaginary_t], axis=1)
    lower = jnp.concatenate([imaginary_t, real_t], axis=1)
    return jnp.concatenate([upper, lower], axis=0)


def propagate(sink_matrix, tau):
    vector_count = sink_matrix.shape[1]
    spin_count = tau.shape[1] // vector_count
    column_count = tau.shape[2]
    real_part, imaginary = (sink_matrix[0], sink_matrix[1])
    upper = jnp.concatenate([real_part, -imaginary], axis=1)
    lower = jnp.concatenate([imaginary, real_part], axis=1)
    sink_big = jnp.concatenate([upper, lower], axis=0)
    stacked = jnp.transpose(tau.reshape(2, spin_count, vector_count, column_count), (0, 2, 1, 3))
    stacked = stacked.reshape(2 * vector_count, spin_count * column_count)
    product = jnp.dot(sink_big, stacked, preferred_element_type=jnp.float32)
    product = jnp.transpose(
        product.reshape(2, vector_count, spin_count, column_count), (0, 2, 1, 3)
    )
    return product.reshape(2, spin_count * vector_count, column_count).astype(jnp.bfloat16)


def attach_source(propagated, source_big):
    vector_count = source_big.shape[0] // 2
    row_count = propagated.shape[1]
    spin_count = propagated.shape[2] // vector_count
    stacked = jnp.concatenate(
        [
            propagated[0].reshape(row_count, spin_count, vector_count),
            propagated[1].reshape(row_count, spin_count, vector_count),
        ],
        axis=2,
    )
    product = jnp.dot(
        stacked.reshape(row_count * spin_count, 2 * vector_count),
        source_big,
        preferred_element_type=jnp.float32,
    )
    product = jnp.transpose(product.reshape(row_count, spin_count, 2, vector_count), (2, 0, 1, 3))
    return product.reshape(2, row_count, spin_count * vector_count)


def general_body(eigenvectors, perambulator, momenta, ratios, source_slice):
    slab_count = eigenvectors.shape[0]
    color_count = eigenvectors.shape[2]
    site_count = eigenvectors.shape[3]
    vector_count = eigenvectors.shape[4]
    first_site = lax.axis_index("space") * site_count
    cosine, sine_part = site_phases(momenta, first_site, site_count)
    normalizer = 1.0 / math.sqrt(color_count * site_count * lax.axis_size("space") * vector_count)
    weights = (
        ratios[:, 0].astype(jnp.float32) / ratios[:, 1].astype(jnp.float32) * normalizer
    ).reshape(1, 2, 1, 1, 1)
    parts = elementals(eigenvectors, cosine, sine_part)
    partial_sums = jnp.sum(weights * parts, axis=1, keepdims=True)
    summed = lax.psum(partial_sums, "space")
    sink_matrices = summed[:, 0].astype(jnp.bfloat16)
    global_slice = source_slice[0] % (slab_count * lax.axis_size("tm"))
    local_source = lax.dynamic_index_in_dim(
        sink_matrices, global_slice % slab_count, 0, keepdims=False
    )
    chosen = spread(local_source, "tm", global_slice // slab_count)
    source_big = source_block(chosen)
    results = []
    for slab in range(slab_count):
        propagated = propagate(sink_matrices[slab], perambulator[slab])[None]
        turned = lax.all_to_all(propagated, "space", split_axis=2, concat_axis=3, tiled=True)
        results.append(attach_source(turned[0], source_big))
    return jnp.stack(results)


HBM = pl.BlockSpec(memory_space=pltpu.MemorySpace.HBM)


def in_hbm(array):
    return pltpu.with_memory_space_constraint(array, pltpu.MemorySpace.HBM)


def pick_kernel(distances, tau_hbm, *refs):
    outs = refs[-3 - len(distances) : -3]
    buffer, in_sems, out_sems = refs[-3:]
    place = lax.axis_index("space")
    pieces = in_sems.shape[1]
    rows = tau_hbm.shape[2] // (pieces // 2)
    loads = []
    stores = []
    for i, out in enumerate(outs):
        for piece in range(pieces):
            part = piece % 2
            some = pl.ds(piece // 2 * rows, rows)
            source = tau_hbm.at[part, place ^ distances[i], some]
            kept = buffer.at[i, part, some]
            loads.append(pltpu.make_async_copy(source, kept, in_sems.at[i, piece]))
            stores.append(
                pltpu.make_async_copy(kept, out.at[part, some], out_sems.at[i, piece])
            )
    for copy in loads:
        copy.start()
    for load, store in zip(loads, stores):
        load.wait()
        store.start()
    for copy in stores:
        copy.wait()


def pick_blocks(tau, distances, after=()):
    _, _, n, columns = tau.shape
    count = len(distances)
    pieces = PIECES
    return pl.pallas_call(
        functools.partial(pick_kernel, distances),
        in_specs=[HBM] + [pl.BlockSpec(memory_space=pl.ANY)] * len(after),
        out_specs=[HBM] * count,
        scratch_shapes=[
            pltpu.VMEM((count, 2, n, columns), tau.dtype),
            pltpu.SemaphoreType.DMA((count, pieces)),
            pltpu.SemaphoreType.DMA((count, pieces)),
        ],
        out_shape=[jax.ShapeDtypeStruct((2, n, columns), tau.dtype)] * count,
        name="pick",
    )(in_hbm(tau), *after)


def elemental_kernel(
    momenta_hbm,
    ratios_hbm,
    v_hbm,
    rounded_a,
    rounded_b,
    full_a,
    full_b,
    vectors,
    table,
    phased,
    total,
    momenta,
    ratios,
    sems,
    small_sems,
):
    place = lax.axis_index("space")
    colors = v_hbm.shape[1]
    site_count = v_hbm.shape[2]
    n = v_hbm.shape[3]
    half = n // 2
    loads = [
        pltpu.make_async_copy(v_hbm.at[:, c], vectors.at[c], sems.at[c]) for c in range(colors)
    ]
    small = [
        pltpu.make_async_copy(momenta_hbm, momenta, small_sems.at[0]),
        pltpu.make_async_copy(ratios_hbm, ratios, small_sems.at[1]),
    ]
    for copy in small + loads:
        copy.start()
    for copy in small:
        copy.wait()

    row = lax.broadcasted_iota(jnp.int32, (8, 128), 0)
    lane = lax.broadcasted_iota(jnp.int32, (8, 128), 1)
    second = (row & 1) == 1
    along = [jnp.where(second, momenta[1, a], momenta[0, a]) for a in range(3)]
    shift = jnp.where((row & 2) == 2, LSIDE - LSIDE // 4, 0)
    for tile in range(site_count // 128):
        site = place * site_count + tile * 128 + lane
        turn = (
            along[0] * (site % LSIDE)
            + along[1] * (site // LSIDE % LSIDE)
            + along[2] * (site // (LSIDE * LSIDE))
            + shift
        )
        turn = turn & (LSIDE - 1)
        angle = turn.astype(jnp.float32) * (2.0 * math.pi / LSIDE)
        table[pl.ds(tile * 128, 128), 0:8] = jnp.cos(angle).T

    def phase(color, k):
        slot = (2 * color + k) % 2
        real = vectors[color, 0].astype(jnp.float32)
        imag = vectors[color, 1].astype(jnp.float32)
        c = table[:, k : k + 1]
        s = table[:, k + 2 : k + 3]
        phased[slot, :, 0:n] = (c * real + s * imag).astype(jnp.bfloat16)
        phased[slot, :, n : 2 * n] = (c * imag - s * real).astype(jnp.bfloat16)

    def multiply(color, k):
        slot = (2 * color + k) % 2
        cols = slice(2 * k * n, (2 * k + 2) * n)
        for part in range(2):
            product = lax.dot_general(
                vectors[color, part],
                phased[slot],
                (((0,), (0,)), ((), ())),
                preferred_element_type=jnp.float32,
            )
            rows = slice(part * n, (part + 1) * n)
            if color == 0:
                total[rows, cols] = product
            else:
                total[rows, cols] += product

    before = None
    for color in range(colors):
        loads[color].wait()
        for k in range(2):
            phase(color, k)
            if before is not None:
                multiply(*before)
            before = (color, k)
    multiply(*before)

    normalizer = 1.0 / math.sqrt(colors * site_count * lax.axis_size("space") * n)
    re = 0.0
    im = 0.0
    for k in range(2):
        ratio = [jnp.full((8, 128), ratios[k, i], jnp.int32).astype(jnp.float32) for i in range(2)]
        w = (ratio[0] / ratio[1] * normalizer)[0:1, 0:1]
        zr = slice((2 * k) * n, (2 * k + 1) * n)
        zi = slice((2 * k + 1) * n, (2 * k + 2) * n)
        re += w * (total[0:n, zr] + total[n : 2 * n, zi])
        im += w * (total[0:n, zi] - total[n : 2 * n, zr])
    for part, value in enumerate((re, im)):
        small = value.astype(jnp.bfloat16)
        rounded_a[part] = small[:half]
        rounded_b[part] = small[half:]
        full_a[part] = value[:half]
        full_b[part] = value[half:]


def elemental_sums(vectors, momenta, ratios):
    _, color_count, site_count, n = vectors.shape
    half = n // 2
    rows = pl.BlockSpec((2, half, n), lambda i: (0, 0, 0))
    return pl.pallas_call(
        elemental_kernel,
        grid=(1,),
        in_specs=[HBM] * 3,
        out_specs=[rows] * 4,
        scratch_shapes=[
                pltpu.VMEM((color_count, 2, site_count, n), jnp.bfloat16),
                pltpu.VMEM((site_count, 128), jnp.float32),
                pltpu.VMEM((2, site_count, 2 * n), jnp.bfloat16),
                pltpu.VMEM((2 * n, 4 * n), jnp.float32),
                pltpu.SMEM(momenta.shape, jnp.int32),
                pltpu.SMEM(ratios.shape, jnp.int32),
                pltpu.SemaphoreType.DMA((color_count,)),
                pltpu.SemaphoreType.DMA((2,)),
        ],
        out_shape=[
            jax.ShapeDtypeStruct((2, half, n), dtype)
            for dtype in (jnp.bfloat16, jnp.bfloat16, jnp.float32, jnp.float32)
        ],
        compiler_params=pltpu.CompilerParams(vmem_limit_bytes=40 * 1024 * 1024),
        name="elementals",
    )(in_hbm(momenta), in_hbm(ratios), in_hbm(vectors))


def complex_rows(real, imag):
    upper = jnp.concatenate([real, imag], axis=1)
    lower = jnp.concatenate([-imag, real], axis=1)
    return jnp.concatenate([upper, lower], axis=0)


def sandwich(sink, tau_re, tau_im, source):
    prop = jnp.dot(sink, complex_rows(tau_re, tau_im), preferred_element_type=jnp.float32)
    return lax.dot_general(
        prop.astype(jnp.bfloat16),
        source,
        (((1,), (1,)), ((), ())),
        preferred_element_type=jnp.float32,
    )


def three_kernel(source_slice, *refs):
    (sink_a, sink_b, here_a, here_b, far_a, far_b, beside_a, beside_b) = refs[:8]
    tau_hbm, got1, got3 = refs[8:11]
    out_hbm, sink_out, source_out = refs[11:14]
    blocks, staged, block_sems, out_sems = refs[14:]
    n = sink_out.shape[0]
    place = lax.axis_index("space")
    time = lax.axis_index("tm")
    same = jnp.where(source_slice[0] % lax.axis_size("tm") // 2 == time // 2, 1, 0)
    odd = time % 2

    pltpu.make_async_copy(tau_hbm.at[:, place], blocks.at[0], block_sems.at[0]).start()
    pltpu.make_async_copy(got1, blocks.at[1], block_sems.at[1]).start()
    pltpu.make_async_copy(got3, blocks.at[2], block_sems.at[2]).start()

    def halves(first, second):
        return jnp.concatenate([first, second], axis=0)

    sink = [halves(sink_a[part], sink_b[part]) for part in range(2)]
    sink_rows = jnp.concatenate(sink, axis=1)
    sink_out[...] = sink_rows

    def away(far, beside, part):
        upper = jnp.where(odd == 0, far[part], beside[part])
        lower = jnp.where(odd == 0, beside[part], far[part])
        return halves(upper, lower)

    source = [
        halves(
            *[
                jnp.where(same == 1, here[part], away(far, beside, part))
                for here, far, beside in ((here_a, far_a, beside_a), (here_b, far_b, beside_b))
            ]
        )
        for part in range(2)
    ]
    source_rows = complex_rows(*source)
    source_out[...] = source_rows

    stores = []
    for i in range(3):
        pltpu.make_async_copy(got1, blocks.at[i], block_sems.at[i]).wait()
        product = sandwich(sink_rows, blocks[i, 0], blocks[i, 1], source_rows)
        staged[i, 0] = product[:, :n]
        staged[i, 1] = product[:, n:]
        column = pl.multiple_of((place ^ (0, 1, 3)[i]) * n, 128)
        store = pltpu.make_async_copy(
            staged.at[i], out_hbm.at[0, :, :, pl.ds(column, n)], out_sems.at[i]
        )
        store.start()
        stores.append(store)
    for store in stores:
        store.wait()


def three_blocks(source_slice, pieces, tau, got, spins):
    n = tau.shape[2]
    return pl.pallas_call(
        three_kernel,
        grid_spec=pltpu.PrefetchScalarGridSpec(
            num_scalar_prefetch=1,
            grid=(1,),
            in_specs=[pl.BlockSpec(piece.shape, lambda i, *_: (0, 0, 0)) for piece in pieces]
            + [HBM] * 3,
            out_specs=[
                HBM,
                pl.BlockSpec((n, 2 * n), lambda i, *_: (0, 0)),
                pl.BlockSpec((2 * n, 2 * n), lambda i, *_: (0, 0)),
            ],
            scratch_shapes=[
                pltpu.VMEM((3, 2, n, n), jnp.bfloat16),
                pltpu.VMEM((3, 2, n, n), jnp.float32),
                pltpu.SemaphoreType.DMA((3,)),
                pltpu.SemaphoreType.DMA((3,)),
            ],
        ),
        out_shape=[
            jax.ShapeDtypeStruct((1, 2, n, spins * n), jnp.float32),
            jax.ShapeDtypeStruct((n, 2 * n), jnp.bfloat16),
            jax.ShapeDtypeStruct((2 * n, 2 * n), jnp.bfloat16),
        ],
        compiler_params=pltpu.CompilerParams(vmem_limit_bytes=40 * 1024 * 1024),
        name="three",
    )(source_slice, *pieces, in_hbm(tau), *got)


def last_kernel(sink, source, got2, _, out_hbm, block, staged, sem, out_sem):
    n = sink.shape[0]
    place = lax.axis_index("space")
    load = pltpu.make_async_copy(got2, block, sem)
    load.start()
    load.wait()
    product = sandwich(sink[...], block[0], block[1], source[...])
    staged[0] = product[:, :n]
    staged[1] = product[:, n:]
    column = pl.multiple_of((place ^ 2) * n, 128)
    store = pltpu.make_async_copy(staged, out_hbm.at[0, :, :, pl.ds(column, n)], out_sem)
    store.start()
    store.wait()


def last_block(sink, source, got2, out):
    n = sink.shape[0]
    return pl.pallas_call(
        last_kernel,
        grid=(1,),
        in_specs=[
            pl.BlockSpec((n, 2 * n), lambda i: (0, 0)),
            pl.BlockSpec((2 * n, 2 * n), lambda i: (0, 0)),
            HBM,
            HBM,
        ],
        out_specs=HBM,
        scratch_shapes=[
            pltpu.VMEM((2, n, n), jnp.bfloat16),
            pltpu.VMEM((2, n, n), jnp.float32),
            pltpu.SemaphoreType.DMA,
            pltpu.SemaphoreType.DMA,
        ],
        out_shape=jax.ShapeDtypeStruct(out.shape, out.dtype),
        input_output_aliases={3: 0},
        compiler_params=pltpu.CompilerParams(vmem_limit_bytes=40 * 1024 * 1024),
        name="last",
    )(sink, source, got2, out)


def xor_pairs(count, bit):
    return [(i, i ^ bit) for i in range(count)]


def block_body(eigenvectors, perambulator, momenta, ratios, source_slice):
    return ordered_body(eigenvectors, perambulator, momenta, ratios, source_slice)


def ordered_body(eigenvectors, perambulator, momenta, ratios, source_slice):
    n = eigenvectors.shape[4]
    quarter = n // 4
    spins = lax.axis_size("space")
    times = lax.axis_size("tm")
    j = lax.axis_index("space")
    inner = (j == 1) | (j == 2)
    odd = lax.axis_index("tm") % 2
    tau = perambulator[0].reshape(2, spins, n, n)

    def move(value, pairs, axis="space"):
        return lax.ppermute(value, axis, pairs)

    middle = [(1, 2), (2, 1)]
    inward = [(0, 1), (3, 2)]
    outward = [(1, 0), (2, 3)]
    core = xor_pairs(times, 1)
    chip = xor_pairs(times, 2)

    (by3,) = pick_blocks(tau, (3,))
    got3 = move(by3, xor_pairs(spins, 3))
    rounded_a, rounded_b, full_a, full_b = elemental_sums(eigenvectors[0], momenta, ratios)
    by1, by2 = pick_blocks(tau, (1, 2), (rounded_b,))
    got1 = move(by1, xor_pairs(spins, 1))
    got2 = move(by2, xor_pairs(spins, 2))

    pieces = []
    for rounded, full in ((rounded_a, full_a), (rounded_b, full_b)):
        inside = move(rounded, inward)
        pair = full + inside.astype(jnp.float32)
        across = move(pair.astype(jnp.bfloat16), middle)
        summed = (pair + across.astype(jnp.float32)).astype(jnp.bfloat16)
        outside = move(summed, outward)
        sink = jnp.where(inner, summed, outside)
        partner = move(sink, core, "tm")
        here = jnp.where(source_slice[0] % 2 == odd, sink, partner)
        mine = lax.dynamic_slice_in_dim(here, odd * quarter, quarter, 1)
        far = move(mine, chip, "tm")
        beside = move(far, core, "tm")
        pieces.append((sink, here, far, beside))
    pieces = [piece for pair in zip(*pieces) for piece in pair]

    out, sink, source = three_blocks(source_slice, pieces, tau, [in_hbm(got) for got in (got1, got3)], spins)
    return last_block(sink, source, got2, out)


def fits(mesh, eigenvectors, perambulator):
    n = eigenvectors.shape[4]
    space = mesh.shape["space"]
    return (
        eigenvectors.shape[0] == mesh.shape["cfg"] * mesh.shape["tm"]
        and space == SPINS
        and mesh.shape["tm"] == 4
        and perambulator.shape[2] == space * n
        and perambulator.shape[3] == space * n
        and eigenvectors.shape[3] % (128 * space) == 0
        and n % 128 == 0
    )


def solution(mesh):
    placed = (
        P(("cfg", "tm"), None, None, "space", None),
        P(("cfg", "tm"), None, None, "space"),
        P(),
        P(),
        P(),
    )

    def mapped(body):
        return jax.shard_map(
            body,
            mesh=mesh,
            in_specs=placed,
            out_specs=P(("cfg", "tm"), None, "space", None),
            check_vma=False,
        )

    def program(*arrays):
        if not fits(mesh, arrays[0], arrays[1]):
            return mapped(general_body)(*arrays)
        return mapped(block_body)(*arrays)

    return program
```
